128 devices in a mesh: row: 16 (over y, z), col: 8 (over x, core).
Axes of the slice: x: 4, y: 4, z: 4, core: 2. Of those that a mesh axis runs over, the one named last changes fastest.
Arguments:
- spectrum: float32 [2, 8192, 4096], P(None, 'row', 'col'), may hold values from -6 to 6
- pupil: float32 [2, 512, 512], replicated, may hold values from -4.2 to 4.2
- amplitudes: float32 [16, 8, 1, 512, 512], P('row', 'col'), may hold values from 0.1 to 3
- offsets: int32 [16, 8, 1, 2], P('row', 'col'), may hold values from 0 to 511, as said below
- counts: int32 [16, 8], P('row', 'col'), may hold values from 1 to 1, as said below
Outputs:
- recovered: float32 [2, 8192, 4096], P(None, 'row', 'col')
The draws below stay inside these ranges and needn't reach their ends.
Inputs may be any that keep to these rules, and one draw needn't show every extreme that they name: `offsets`: offsets are corners inside the tile: the row below 512, the column below 512. `counts`: some device has all 1 slots live.
All inputs are finite; a program needn't handle non-finite values.
Results may differ from the reference program's by a relative error of at most 0.012.
Values sent between devices are 32-bit elements; how exact they have to be, the bound alone decides.
No kernel may reach another device: no remote copies, remote signals or barrier semaphores. Data moves between devices by JAX's collectives and lax.ppermute only.
A program may use at most 128 MiB of HBM per device.

```python
import math
import jax
import jax.numpy as jnp
from jax import lax

W = 512
TR = 512
TC = 512
CAP = 1
SWEEPS = 2
NR = 8192
NC = 4096
N_ROW = 16
N_COL = 8


def draw_offsets(key, part):
    first = jax.random.randint(jax.random.fold_in(key, 11), (N_ROW, N_COL, CAP, 1), 0, TR)
    second = jax.random.randint(jax.random.fold_in(key, 12), (N_ROW, N_COL, CAP, 1), 0, TC)
    return jnp.concatenate([first, second], axis=3).astype(jnp.int32)


def draw_counts(key, part):
    base = jax.random.randint(jax.random.fold_in(key, 21), (N_ROW * N_COL,), 1, CAP + 1)
    chosen = jax.random.randint(jax.random.fold_in(key, 22), (), 0, N_ROW * N_COL)
    base = base.at[chosen].set(CAP)
    return base.reshape(N_ROW, N_COL).astype(jnp.int32)


def levels(own_key, dims, pieces, least, top_value):
    factor_of, own = 1.0, jax.random.fold_in(own_key, 6)
    for axis_at, blocks in pieces:
        draws = jnp.exp(jax.random.uniform(jax.random.fold_in(own, axis_at), (blocks,), jnp.float32, least / len(pieces), top_value / len(pieces)))
        factor_of = factor_of * jnp.repeat(draws, dims[axis_at] // blocks).reshape([-1 if axis == axis_at else 1 for axis in range(len(dims))])
    return factor_of


def normal_values(own_key, extent, scale, limit, shards=(), kind=jnp.bfloat16):
    drawn = scale * jax.random.normal(own_key, extent, jnp.float32)
    if shards:
        drawn = drawn * levels(own_key, extent, shards, -0.22, 0.18)
    return jnp.clip(drawn, -limit, limit).astype(kind)


def setup_inputs(seed: int = 0) -> dict:
    key_list = jax.random.split(jax.random.key(seed), 6)
    spectrum = normal_values(key_list[0], (2, NR, NC), 1.0, 6.0, ((1, 16), (2, 8)), jnp.float32)
    pupil = normal_values(key_list[1], (2, W, W), 0.7, 4.2, (), jnp.float32)
    amplitudes = jnp.clip(jnp.exp(math.log(3.0) - 3.4011974 * jax.random.uniform(key_list[2], (N_ROW, N_COL, CAP, W, W), jnp.float32) ** levels(key_list[2], (N_ROW, N_COL, CAP, W, W), ((0, 16), (1, 8)), -0.2, 0.2)), 0.1, 3.0)
    offsets = draw_offsets(jax.random.fold_in(key_list[5], 71), 0)
    counts = draw_counts(jax.random.fold_in(key_list[5], 71), 0)
    return {"spectrum": spectrum, "pupil": pupil, "amplitudes": amplitudes, "offsets": offsets, "counts": counts}


step_size = 0.5
floor_value = 0.05

def dft_tables(width):
    index = jnp.arange(width, dtype=jnp.int32)
    phase = index[:, None] * index[None, :] % width
    angle = phase.astype(jnp.float32) * (2.0 * math.pi / width)
    scale = 1.0 / math.sqrt(width)
    return ((jnp.cos(angle) * scale).astype(jnp.bfloat16), (jnp.sin(angle) * scale).astype(jnp.bfloat16))

def transform(real, imag, cosine, sine, sign):
    cosine = cosine.astype(jnp.float32)
    sine = sine.astype(jnp.float32)
    real = real.astype(jnp.bfloat16).astype(jnp.float32)
    imag = imag.astype(jnp.bfloat16).astype(jnp.float32)

    def right(a, b):
        return jnp.einsum('swk,kj->swj', a, b, precision=lax.Precision.HIGHEST)

    def left(b, a):
        return jnp.einsum('ik,skj->sij', b, a, precision=lax.Precision.HIGHEST)
    first_real = (right(real, cosine) - sign * right(imag, sine)).astype(jnp.bfloat16).astype(jnp.float32)
    first_imag = (right(imag, cosine) + sign * right(real, sine)).astype(jnp.bfloat16).astype(jnp.float32)
    out_real = left(cosine, first_real) - sign * left(sine, first_imag)
    out_imag = left(cosine, first_imag) + sign * left(sine, first_real)
    return (out_real, out_imag)

def slot_gradient(window_real, window_imag, pupil, amps, live, cosine, sine):
    pupil_real = pupil[0][None]
    pupil_imag = pupil[1][None]
    field_real = window_real * pupil_real - window_imag * pupil_imag
    field_imag = window_real * pupil_imag + window_imag * pupil_real
    wave_real, wave_imag = transform(field_real, field_imag, cosine, sine, 1.0)
    magnitude = jnp.sqrt(wave_real * wave_real + wave_imag * wave_imag)
    keep = 1.0 - amps / jnp.maximum(magnitude, floor_value)
    back_real, back_imag = transform(wave_real * keep, wave_imag * keep, cosine, sine, -1.0)
    mask = live[:, None, None]
    grad_real = (back_real * pupil_real + back_imag * pupil_imag) * mask
    grad_imag = (back_imag * pupil_real - back_real * pupil_imag) * mask
    return (grad_real, grad_imag)

def reference(spectrum, pupil, amplitudes, offsets, counts):
    cosine, sine = dft_tables(W)
    total_slots = N_ROW * N_COL * CAP
    flat_amps = amplitudes.reshape(total_slots, W, W)
    flat_offsets = offsets.reshape(total_slots, 2)
    flat_counts = counts.reshape(N_ROW * N_COL)
    for sweep in range(SWEEPS):
        padded = jnp.pad(spectrum, ((0, 0), (0, W), (0, W)))

        def one(index, total):
            device = index // CAP
            slot = index % CAP
            row_start = (device // N_COL * TR + flat_offsets[index, 0]).astype(jnp.int32)
            col_start = (device % N_COL * TC + flat_offsets[index, 1]).astype(jnp.int32)
            zero = jnp.zeros((), jnp.int32)
            window = lax.dynamic_slice(padded, (zero, row_start, col_start), (2, W, W))
            amp = lax.dynamic_slice_in_dim(flat_amps, index.astype(jnp.int32), 1, 0)
            live = (slot < flat_counts[device]).astype(jnp.float32)
            grad_real, grad_imag = slot_gradient(window[0][None], window[1][None], pupil, amp, live[None], cosine, sine)
            piece = jnp.stack([grad_real[0], grad_imag[0]])
            current = lax.dynamic_slice(total, (zero, row_start, col_start), (2, W, W))
            return lax.dynamic_update_slice(total, current + piece, (zero, row_start, col_start))
        total = lax.fori_loop(jnp.int32(0), jnp.int32(total_slots), one, jnp.zeros_like(padded))
        spectrum = spectrum - step_size * total[:, :NR, :NC]
    return spectrum
```

```python
import functools
import math

import jax
import jax.numpy as jnp
from jax import lax
from jax.experimental import pallas as pl
from jax.experimental.pallas import tpu as pltpu
from jax.sharding import PartitionSpec as P

STEP = 0.5
FLOOR = 0.05
VMEM = pl.BlockSpec(memory_space=pltpu.VMEM)
SMEM = pl.BlockSpec(memory_space=pltpu.SMEM)
LIMIT = 48 * 1024 * 1024
CHUNKS = (128, 128, 128, 128)

OY, OX, OYA, OXA, OYB, OXB, OYL, OYR, EDGE_Y, EDGE_X, LIVE = range(11)


def shifted(value, axis, steps):
    count = lax.axis_size(axis)
    leading, last = (max(0, -steps), min(count, count - steps))
    return lax.ppermute(value, axis, [(source, source + steps) for source in range(leading, last)])


def dft_tables(width):
    index = jnp.arange(width, dtype=jnp.int32)
    phase = index[:, None] * index[None, :] % width
    angle = phase.astype(jnp.float32) * (2.0 * math.pi / width)
    scale = 1.0 / math.sqrt(width)
    return (
        (jnp.cos(angle) * scale).astype(jnp.bfloat16),
        (jnp.sin(angle) * scale).astype(jnp.bfloat16),
    )


def call(kernel, outs, arrays, scalars, scratch=()):
    return pl.pallas_call(
        kernel,
        out_shape=outs,
        in_specs=[SMEM] + [VMEM] * len(arrays),
        out_specs=jax.tree.map(lambda _: VMEM, outs),
        scratch_shapes=list(scratch),
        compiler_params=pltpu.CompilerParams(vmem_limit_bytes=LIMIT),
    )(scalars, *arrays)


def rows_of(shape, first):
    return lax.broadcasted_iota(jnp.int32, shape, 0) + first


def cols_of(shape):
    return lax.broadcasted_iota(jnp.int32, shape, 1)


def prepare_kernel(sc, cos_ref, sin_ref, pupil_ref, bx, bxt, by, byt, pupil_out):
    w = cos_ref.shape[0]
    cosine = cos_ref[...].astype(jnp.float32)
    sine = sin_ref[...].astype(jnp.float32)
    for shift, plain, flipped in ((sc[OX], bx, bxt), (sc[OY], by, byt)):
        for axis, out, sign in ((0, plain, 1.0), (1, flipped, -1.0)):
            c = pltpu.roll(cosine, shift, axis).astype(jnp.bfloat16)
            s = (pltpu.roll(sine, shift, axis) * sign).astype(jnp.bfloat16)
            out[:w, :w] = c
            out[w:, w:] = c
            out[:w, w:] = s
            out[w:, :w] = -s
    for part in range(2):
        pupil_out[part] = pltpu.roll(pltpu.roll(pupil_ref[part], sc[OY], 0), sc[OX], 1)


def gradient(sc, window, pupil, amp, bx, bxt, by, byt, outs, firsts, left, stacked, extra):
    w = amp.shape[0]
    for first, size in firsts:
        rows = pl.ds(first, size)
        wr, wi = window(first, size)
        pr, pi = pupil[0, rows, :], pupil[1, rows, :]
        left[rows, :w] = (wr * pr - wi * pi).astype(jnp.bfloat16)
        left[rows, w:] = (wr * pi + wi * pr).astype(jnp.bfloat16)

    def dot(a, b):
        return jnp.dot(a, b, preferred_element_type=jnp.float32)

    stacked[:w, :] = dot(left[...], bx[:, :w]).astype(jnp.bfloat16)
    stacked[w:, :] = dot(left[...], bx[:, w:]).astype(jnp.bfloat16)
    live = (sc[LIVE] > 0).astype(jnp.float32)
    block = 128
    for first in range(0, w, block):
        rows = pl.ds(first, block)
        wave_r = dot(byt[rows, :], stacked[...])
        wave_i = dot(byt[pl.ds(w + first, block), :], stacked[...])
        power = jnp.maximum(wave_r * wave_r + wave_i * wave_i, FLOOR * FLOOR)
        keep = (1.0 - amp[rows, :] * lax.rsqrt(power)) * live
        left[rows, :w] = (wave_r * keep).astype(jnp.bfloat16)
        left[rows, w:] = (wave_i * keep).astype(jnp.bfloat16)
    stacked[:w, :] = dot(left[...], bxt[:, :w]).astype(jnp.bfloat16)
    stacked[w:, :] = dot(left[...], bxt[:, w:]).astype(jnp.bfloat16)
    for index, (first, size) in enumerate(firsts):
        rows = pl.ds(first, size)
        back_r = dot(by[rows, :], stacked[...])
        back_i = dot(by[pl.ds(w + first, size), :], stacked[...])
        pr, pi = pupil[0, rows, :], pupil[1, rows, :]
        grad_r = back_r * pr + back_i * pi
        grad_i = back_i * pr - back_r * pi
        if extra is not None:
            grad_r = grad_r + extra[index][0]
            grad_i = grad_i + extra[index][1]
        outs[index][0] = grad_r
        outs[index][1] = grad_i


def first_kernel(n, firsts, sc, tile, *refs):
    below, right = refs[:n], refs[n : 2 * n]
    pupil, amp, bx, bxt, by, byt = refs[2 * n : 2 * n + 6]
    outs, (kept, left, stacked) = refs[2 * n + 6 : 3 * n + 6], refs[3 * n + 6 :]

    def window(first, size):
        index = [f for f, _ in firsts].index(first)
        shape = (size, tile.shape[2])
        low = rows_of(shape, first) < sc[OY]
        far = cols_of(shape) < sc[OX]
        parts = []
        for part in range(2):
            near = jnp.where(low, below[index][part], tile[part, pl.ds(first, size), :])
            value = jnp.where(far, right[index][part], near)
            kept[part, pl.ds(first, size), :] = value
            parts.append(value)
        return parts

    gradient(sc, window, pupil, amp, bx, bxt, by, byt, outs, firsts, left, stacked, None)


def second_kernel(n, firsts, sc, kept, *refs):
    own, from_left, from_right, grads = (refs[k * n : (k + 1) * n] for k in range(4))
    pupil, amp, bx, bxt, by, byt = refs[4 * n : 4 * n + 6]
    outs, (left, stacked) = refs[4 * n + 6 : 5 * n + 6], refs[5 * n + 6 :]

    def window(first, size):
        index = [f for f, _ in firsts].index(first)
        shape = (size, kept.shape[2])
        rows, cols = rows_of(shape, first), cols_of(shape)
        far = cols < sc[OX]
        inside = (rows >= sc[EDGE_Y]) & (cols >= sc[EDGE_X])
        parts = []
        for part in range(2):
            near = jnp.where(far, from_right[index][part], from_left[index][part])
            value = kept[part, pl.ds(first, size), :] - STEP * (own[index][part] + near)
            parts.append(jnp.where(inside, value, 0.0))
        return parts

    gradient(sc, window, pupil, amp, bx, bxt, by, byt, outs, firsts, left, stacked, grads)


def compose_kernel(first, sc, tile, below, out):
    shape = tile.shape[1:]
    low = rows_of(shape, first) < sc[OYL]
    for part in range(2):
        out[part] = jnp.where(low, below[part], tile[part])


def between_kernel(first, sc, mine, above, below, to_left, to_right, own):
    shape = mine.shape[1:]
    i, j = rows_of(shape, first), cols_of(shape)
    low, low_a, low_b = i < sc[OY], i < sc[OYA], i < sc[OYB]
    far, far_a, far_b = j < sc[OX], j < sc[OXA], j < sc[OXB]
    low_l, low_r = i < sc[OYL], i < sc[OYR]
    zero = jnp.zeros(shape, jnp.float32)

    def seen(low_x):
        same = low == low_x
        return same, ~low_x & low_a, low_x & ~low_b

    left_m = [a & ~b for a, b in zip(seen(low_l), (far, far_a, far_b))]
    right_m = [a & b for a, b in zip(seen(low_r), (far, far_a, far_b))]
    _, own_a, own_b = seen(low)
    own_a, own_b = own_a & (far == far_a), own_b & (far == far_b)
    for part in range(2):
        values = (mine[part], above[part], below[part])
        for out, masks in ((to_left, left_m), (to_right, right_m)):
            terms = [jnp.where(m, v, zero) for m, v in zip(masks, values)]
            out[part] = terms[0] + terms[1] + terms[2]
        own[part] = values[0] + jnp.where(own_a, values[1], zero) + jnp.where(own_b, values[2], zero)


def final_kernel(first, sc, tile, mine, above, to_right, base):
    shape = mine.shape[1:]
    i, j = rows_of(shape, first), cols_of(shape)
    stay, come = i >= sc[OY], i < sc[OYA]
    far, far_a = j < sc[OX], j < sc[OXA]
    zero = jnp.zeros(shape, jnp.float32)
    for part in range(2):
        own = jnp.where(stay, mine[part], zero)
        other = jnp.where(come, above[part], zero)
        to_right[part] = jnp.where(far, own, zero) + jnp.where(far_a, other, zero)
        kept = jnp.where(far, zero, own) + jnp.where(far_a, zero, other)
        base[part] = tile[part] - STEP * kept


def on_device(spectrum, pupil, amplitudes, offsets, counts):
    w = pupil.shape[1]
    amp = amplitudes[0, 0, 0]
    f32 = jnp.float32
    spans, first = [], 0
    for size in CHUNKS:
        spans.append((first, size))
        first += size
    n = len(spans)
    piece = [jax.ShapeDtypeStruct((2, size, w), f32) for _, size in spans]
    whole = jax.ShapeDtypeStruct((2, w, w), f32)

    tiles = [spectrum[:, first : first + size] for first, size in spans]
    below = [shifted(t, "row", -1) for t in tiles]
    place = offsets[0, 0]
    from_left = shifted(place, "col", 1)
    from_right = shifted(place, "col", -1)
    from_above = shifted(place, "row", 1)
    from_below = shifted(place, "row", -1)
    last_row = lax.axis_index("row") == lax.axis_size("row") - 1
    last_col = lax.axis_index("col") == lax.axis_size("col") - 1
    sc = jnp.stack(
        [
            place[0, 0],
            place[0, 1],
            from_above[0, 0],
            from_above[0, 1],
            from_below[0, 0],
            from_below[0, 1],
            from_left[0, 0],
            from_right[0, 0],
            jnp.where(last_row, place[0, 0], 0),
            jnp.where(last_col, place[0, 1], 0),
            counts[0, 0],
        ]
    ).astype(jnp.int32)
    cosine, sine = dft_tables(w)
    table = jax.ShapeDtypeStruct((2 * w, 2 * w), jnp.bfloat16)
    *tables, rolled = call(
        prepare_kernel, [table, table, table, table, whole], (cosine, sine, pupil), sc
    )

    composed = [
        call(functools.partial(compose_kernel, spans[k][0]), piece[k], (tiles[k], below[k]), sc)
        for k in range(n)
    ]
    right = [shifted(c, "col", -1) for c in composed]
    scratch = [pltpu.VMEM((w, 2 * w), jnp.bfloat16), pltpu.VMEM((2 * w, w), jnp.bfloat16)]
    *grads, kept = call(
        functools.partial(first_kernel, n, spans),
        piece + [whole],
        (spectrum, *below, *right, rolled, amp, *tables),
        sc,
        scratch,
    )

    above = [shifted(g, "row", 1) for g in grads]
    under = [shifted(g, "row", -1) for g in grads]
    mixed = [
        call(
            functools.partial(between_kernel, spans[k][0]),
            [piece[k]] * 3,
            (grads[k], above[k], under[k]),
            sc,
        )
        for k in range(n)
    ]
    got_right = [shifted(m[0], "col", -1) for m in mixed]
    got_left = [shifted(m[1], "col", 1) for m in mixed]
    sums = call(
        functools.partial(second_kernel, n, spans),
        piece,
        (kept, *[m[2] for m in mixed], *got_left, *got_right, *grads, rolled, amp, *tables),
        sc,
        scratch,
    )

    above = [shifted(s, "row", 1) for s in sums]
    done = [
        call(
            functools.partial(final_kernel, spans[k][0]),
            [piece[k]] * 2,
            (tiles[k], sums[k], above[k]),
            sc,
        )
        for k in range(n)
    ]
    got = [shifted(d[0], "col", 1) for d in done]
    return jnp.concatenate([d[1] - STEP * g for d, g in zip(done, got)], axis=1)


def solution(mesh):
    in_specs = (
        P(None, "row", "col"),
        P(),
        P("row", "col", None, None, None),
        P("row", "col", None, None),
        P("row", "col"),
    )
    out_specs = P(None, "row", "col")
    return jax.shard_map(
        on_device, mesh=mesh, in_specs=in_specs, out_specs=out_specs, check_vma=False
    )
```

```python
import functools
import math

import jax
import jax.numpy as jnp
from jax import lax
from jax.experimental import pallas as pl
from jax.experimental.pallas import tpu as pltpu
from jax.sharding import PartitionSpec as P

STEP = 0.5
FLOOR = 0.05
VMEM = pl.BlockSpec(memory_space=pltpu.VMEM)
ANY = pl.BlockSpec(memory_space=pl.ANY)
SMEM = pl.BlockSpec(memory_space=pltpu.SMEM)
LIMIT = 12 * 1024 * 1024
F32 = jnp.float32
BF16 = jnp.bfloat16

EXTRA = 8
HEAD = 224


def shifted(value, axis, steps):
    count = lax.axis_size(axis)
    leading, last = (max(0, -steps), min(count, count - steps))
    return lax.ppermute(value, axis, [(source, source + steps) for source in range(leading, last)])


def dft_tables(width):
    index = jnp.arange(width, dtype=jnp.int32)
    phase = index[:, None] * index[None, :] % width
    angle = phase.astype(jnp.float32) * (2.0 * math.pi / width)
    scale = 1.0 / math.sqrt(width)
    return (
        (jnp.cos(angle) * scale).astype(jnp.bfloat16),
        (jnp.sin(angle) * scale).astype(jnp.bfloat16),
    )


def call(kernel, outs, arrays, scratch=(), scalars=(), after=()):
    skip = len(after)

    def body(*refs):
        kernel(*refs[skip:])

    return pl.pallas_call(
        body,
        out_shape=outs,
        in_specs=[ANY] * skip + [SMEM] * len(scalars) + [VMEM] * len(arrays),
        out_specs=jax.tree.map(lambda _: VMEM, outs),
        scratch_shapes=list(scratch),
        compiler_params=pltpu.CompilerParams(vmem_limit_bytes=LIMIT),
    )(*after, *scalars, *arrays)


def indices(shape, first):
    return (
        lax.broadcasted_iota(jnp.int32, shape, 0) + first,
        lax.broadcasted_iota(jnp.int32, shape, 1),
    )


def low(i, place):
    return i + 1 < place[0, :1, :].astype(jnp.int32)


def far(j, place):
    return j + 1 < place[1, :1, :].astype(jnp.int32)


def absent(place):
    return place[0, :1, :] == 0.0


def prepare_kernel(offset, cos_ref, sin_ref, pupil_ref, bx, bxt, by, byt_head, byt_tail, pupil_out):
    w = cos_ref.shape[0]
    h = HEAD
    cosine = cos_ref[...].astype(F32)
    sine = sin_ref[...].astype(F32)
    oy, ox = offset[0, 0], offset[0, 1]

    def rolled(value, shift, axis):
        return pltpu.roll(value, shift, axis)

    c, s = rolled(cosine, ox, 0).astype(BF16), rolled(sine, ox, 0).astype(BF16)
    bx[:w, :w], bx[:w, w:], bx[w:, :w], bx[w:, w:] = c, s, -s, c
    c, s = rolled(cosine, ox, 1).astype(BF16), rolled(sine, ox, 1).astype(BF16)
    bxt[:w, :w], bxt[:w, w:], bxt[w:, :w], bxt[w:, w:] = c, -s, s, c
    c, s = rolled(cosine, oy, 0).astype(BF16), rolled(sine, oy, 0).astype(BF16)
    by[:w, :w], by[:w, w:], by[w:, :w], by[w:, w:] = c, s, -s, c
    c, s = rolled(cosine, oy, 1).astype(BF16), rolled(sine, oy, 1).astype(BF16)
    for out, part in ((byt_head, slice(0, h)), (byt_tail, slice(h, w))):
        n = part.stop - part.start
        out[:w, :n], out[:w, n:] = c[:, part], -s[:, part]
        out[w:, :n], out[w:, n:] = s[:, part], c[:, part]
    for part in range(2):
        pupil_out[part] = rolled(rolled(pupil_ref[part], oy, 0), ox, 1)


def dot(a, b):
    return jnp.dot(a, b, preferred_element_type=F32)


def right_product(first, window, pupil, bx, left, half):
    w = bx.shape[0] // 2
    h = half.shape[0] // 2
    wr, wi = window
    rows = pl.ds(first, h)
    pr, pi = pupil[0, rows, :], pupil[1, rows, :]
    left[:, :w] = (wr * pr - wi * pi).astype(BF16)
    left[:, w:] = (wr * pi + wi * pr).astype(BF16)
    half[:h, :] = dot(left[...], bx[:, :w]).astype(BF16)
    half[h:, :] = dot(left[...], bx[:, w:]).astype(BF16)


def finish(acc, byt_tail, half, amp, live, bxt, left, stacked):
    w = amp.shape[0]
    block = 128
    alive = (live[0, 0] > 0).astype(F32)
    for first in range(0, w, block):
        rows = pl.ds(first, block)
        wave_r = acc[rows, :] + dot(byt_tail[rows, :], half[...])
        shifted_rows = pl.ds(w + first, block)
        wave_i = acc[shifted_rows, :] + dot(byt_tail[shifted_rows, :], half[...])
        power = jnp.maximum(wave_r * wave_r + wave_i * wave_i, FLOOR * FLOOR)
        keep = (1.0 - amp[rows, :] * lax.rsqrt(power)) * alive
        left[rows, :w] = (wave_r * keep).astype(BF16)
        left[rows, w:] = (wave_i * keep).astype(BF16)
    stacked[:w, :] = dot(left[...], bxt[:, :w]).astype(BF16)
    stacked[w:, :] = dot(left[...], bxt[:, w:]).astype(BF16)


def back(first, by, stacked, pupil, out, extra):
    w = stacked.shape[1]
    size = out.shape[1]
    rows = pl.ds(first, size)
    back_r = dot(by[rows, :], stacked[...])
    back_i = dot(by[pl.ds(w + first, size), :], stacked[...])
    pr, pi = pupil[0, rows, :], pupil[1, rows, :]
    grad_r = back_r * pr + back_i * pi
    grad_i = back_i * pr - back_r * pi
    if extra is not None:
        grad_r = grad_r + extra[0]
        grad_i = grad_i + extra[1]
    out[0] = grad_r
    out[1] = grad_i


def gathered(first, head, place, tile, one, both):
    h = both.shape[1]
    i, j = indices(both.shape[1:], first)
    a, b = low(i, place), far(j, place)
    if not head:
        a, b = b, a
    return [jnp.where(b, both[p], jnp.where(a, one[p, :h, :], tile[p, :h, :])) for p in range(2)]


def updated(first, head, place, edge_row, edge_col, kept, own, minus, plus):
    i, j = indices(kept.shape[1:], first)
    a, b = low(i, place), far(j, place)
    outside = (a & absent(edge_row)) | (b & absent(edge_col))
    second = b if head else a
    parts = []
    for p in range(2):
        near = jnp.where(second, plus[p], minus[p])
        parts.append(jnp.where(outside, 0.0, kept[p] - STEP * (own[p] + near)))
    return parts


def open_first(first, place, tile, one, both, pupil, bx, byt, kept, acc, left, half):
    window = gathered(first, True, place, tile, one, both)
    kept[0], kept[1] = window
    right_product(first, window, pupil, bx, left, half)
    acc[...] = dot(byt[...], half[...])


def close_first(
    first, live, place, tile, one, both, acc, pupil, amp, bx, byt, bxt, by, kept, stacked, out, left, half
):
    window = gathered(first, False, place, tile, one, both)
    kept[0], kept[1] = window
    right_product(first, window, pupil, bx, left.at[: half.shape[0] // 2], half)
    finish(acc, byt, half, amp, live, bxt, left, stacked)
    back(0, by, stacked, pupil, out, None)


def open_second(
    first, place, edge_row, edge_col, kept, own, minus, plus, pupil, bx, byt, acc, left, half
):
    window = updated(first, True, place, edge_row, edge_col, kept, own, minus, plus)
    right_product(first, window, pupil, bx, left, half)
    acc[...] = dot(byt[...], half[...])


def close_second(
    first, live, place, edge_row, edge_col, kept, own, minus, plus, acc, pupil, amp, bx, byt, bxt, by,
    extra, stacked, out, left, half
):
    window = updated(first, False, place, edge_row, edge_col, kept, own, minus, plus)
    right_product(first, window, pupil, bx, left.at[: half.shape[0] // 2], half)
    finish(acc, byt, half, amp, live, bxt, left, stacked)
    back(0, by, stacked, pupil, out, extra)


def rest_first(first, by, stacked, pupil, out):
    back(first, by, stacked, pupil, out, None)


def rest_second(first, by, stacked, pupil, extra, out):
    back(first, by, stacked, pupil, out, extra)


def compose_kernel(first, head, target, tile, one, out, place):
    h = out.shape[1]
    i, j = indices(out.shape[1:], first)
    mask = low(i, target) if head else far(j, target)
    for p in range(2):
        out[p] = jnp.where(mask, one[p, :h, :], tile[p, :h, :])
        place[p] = one[p, h:, :]


def between_kernel(
    first, head, me, minus, plus, target_minus, target_plus, mine, got_minus, got_plus, to_minus, to_plus, own
):
    i, j = indices(mine.shape[1:], first)
    ways = (functools.partial(low, i), functools.partial(far, j))
    if not head:
        ways = ways[::-1]
    f, f_minus, f_plus = (ways[0](x) for x in (me, minus, plus))
    s, s_minus, s_plus = (ways[1](x) for x in (me, minus, plus))

    def seen(goal):
        return f == goal, ~goal & f_minus, goal & ~f_plus

    minus_m = [a & ~b for a, b in zip(seen(ways[0](target_minus)), (s, s_minus, s_plus))]
    plus_m = [a & b for a, b in zip(seen(ways[0](target_plus)), (s, s_minus, s_plus))]
    _, own_minus, own_plus = seen(f)
    own_minus, own_plus = own_minus & (s == s_minus), own_plus & (s == s_plus)
    for p in range(2):
        values = (mine[p], got_minus[p], got_plus[p])
        for out, masks in ((to_minus, minus_m), (to_plus, plus_m)):
            terms = [jnp.where(m, v, 0.0) for m, v in zip(masks, values)]
            out[p] = terms[0] + terms[1] + terms[2]
        own[p] = values[0] + jnp.where(own_minus, values[1], 0.0) + jnp.where(own_plus, values[2], 0.0)


def final_kernel(first, head, me, minus, tile, mine, got, to_plus, base):
    h = mine.shape[1]
    i, j = indices(mine.shape[1:], first)
    ways = (functools.partial(low, i), functools.partial(far, j))
    if not head:
        ways = ways[::-1]
    f, f_minus = ways[0](me), ways[0](minus)
    s, s_minus = ways[1](me), ways[1](minus)
    for p in range(2):
        own = jnp.where(f, 0.0, mine[p])
        other = jnp.where(f_minus, got[p], 0.0)
        to_plus[p] = jnp.where(s, own, 0.0) + jnp.where(s_minus, other, 0.0)
        kept = jnp.where(s, 0.0, own) + jnp.where(s_minus, 0.0, other)
        base[p] = tile[p, :h, :] - STEP * kept


def store_kernel(first, base, got, *rest):
    out, value, sem = rest[-3:]
    for p in range(2):
        value[p] = base[p] - STEP * got[p]
    copy = pltpu.make_async_copy(value, out.at[:, pl.ds(first, value.shape[1]), :], sem)
    copy.start()
    copy.wait()


def store(first, base, got, whole, previous=None):
    _, h, w = base.shape
    held = () if previous is None else (previous,)
    return pl.pallas_call(
        functools.partial(store_kernel, first),
        out_shape=whole,
        in_specs=[VMEM, VMEM] + [ANY] * len(held),
        out_specs=ANY,
        scratch_shapes=[pltpu.VMEM((2, h, w), F32), pltpu.SemaphoreType.DMA],
        input_output_aliases={2: 0} if held else {},
        compiler_params=pltpu.CompilerParams(vmem_limit_bytes=LIMIT),
    )(base, got, *held)


def on_device(spectrum, pupil, amplitudes, offsets, counts):
    w = pupil.shape[1]
    h = HEAD
    amp = amplitudes[0, 0, 0]
    offset = offsets[0, 0]
    piece = jax.ShapeDtypeStruct((2, h, w), F32)
    rest = jax.ShapeDtypeStruct((2, w - h, w), F32)
    whole = jax.ShapeDtypeStruct((2, w, w), F32)
    spot = jax.ShapeDtypeStruct((2, EXTRA, w), F32)
    me = jnp.broadcast_to((offset[0] + 1).astype(F32)[:, None, None], (2, EXTRA, w))
    head = jnp.concatenate([spectrum[:, :h], me], axis=1)
    tail = jnp.concatenate([spectrum[:, h:], me], axis=1)

    head_below = shifted(head, "row", -1)
    tail_right = shifted(tail, "col", -1)
    above = shifted(me, "row", 1)
    left_of = shifted(me, "col", 1)

    cosine, sine = dft_tables(w)
    table = jax.ShapeDtypeStruct((2 * w, 2 * w), BF16)
    narrow = [jax.ShapeDtypeStruct((2 * w, 2 * n), BF16) for n in (h, w - h)]
    bx, bxt, by, byt_head, byt_tail, rolled = call(
        prepare_kernel, [table, table, table, *narrow, whole], (cosine, sine, pupil), scalars=(offset,)
    )

    tail_made, right_of = call(
        functools.partial(compose_kernel, h, False), [rest, spot], (above, tail, tail_right)
    )
    tail_both = shifted(tail_made, "row", -1)
    head_made, under = call(
        functools.partial(compose_kernel, 0, True),
        [piece, spot],
        (left_of, head, head_below),
        after=(tail_made,),
    )
    head_both = shifted(head_made, "col", -1)

    total = jax.ShapeDtypeStruct((2 * w, w), F32)
    stack = jax.ShapeDtypeStruct((2 * w, w), BF16)
    half, half_tail = (pltpu.VMEM((2 * n, w), BF16) for n in (h, w - h))
    left_half, left_whole = pltpu.VMEM((h, 2 * w), BF16), pltpu.VMEM((w, 2 * w), BF16)
    head_kept, acc = call(
        functools.partial(open_first, 0),
        [piece, total],
        (me, head, head_below, head_both, rolled, bx, byt_head),
        (left_half, half),
    )
    tail_kept, stacked, head_grad = call(
        functools.partial(close_first, h),
        [rest, stack, piece],
        (me, tail, tail_right, tail_both, acc, rolled, amp, bx, byt_tail, bxt, by),
        (left_whole, half_tail),
        scalars=(counts,),
    )

    got_above, got_under = shifted(head_grad, "row", 1), shifted(head_grad, "row", -1)
    tail_grad = call(functools.partial(rest_first, h), rest, (by, stacked, rolled))
    got_left, got_right = shifted(tail_grad, "col", 1), shifted(tail_grad, "col", -1)
    to_up, to_down, tail_own = call(
        functools.partial(between_kernel, h, False),
        [rest] * 3,
        (me, left_of, right_of, above, under, tail_grad, got_left, got_right),
    )
    tail_sums = (tail_own, shifted(to_down, "row", 1), shifted(to_up, "row", -1))
    to_left, to_right, head_own = call(
        functools.partial(between_kernel, 0, True),
        [piece] * 3,
        (me, above, under, left_of, right_of, head_grad, got_above, got_under),
        after=(to_up,),
    )
    head_sums = (head_own, shifted(to_right, "col", 1), shifted(to_left, "col", -1))

    acc = call(
        functools.partial(open_second, 0),
        total,
        (me, under, right_of, head_kept, *head_sums, rolled, bx, byt_head),
        (left_half, half),
    )
    stacked, head_total = call(
        functools.partial(close_second, h),
        [stack, piece],
        (me, under, right_of, tail_kept, *tail_sums, acc, rolled, amp, bx, byt_tail, bxt, by, head_grad),
        (left_whole, half_tail),
        scalars=(counts,),
    )

    head_above = shifted(head_total, "row", 1)
    tail_total = call(functools.partial(rest_second, h), rest, (by, stacked, rolled, tail_grad))
    tail_left = shifted(tail_total, "col", 1)
    tail_down, tail_base = call(
        functools.partial(final_kernel, h, False), [rest] * 2, (me, left_of, tail, tail_total, tail_left)
    )
    tail_got = shifted(tail_down, "row", 1)
    head_right, head_base = call(
        functools.partial(final_kernel, 0, True),
        [piece] * 2,
        (me, above, head, head_total, head_above),
        after=(tail_down,),
    )
    head_got = shifted(head_right, "col", 1)
    partial = store(0, head_base, head_got, whole)
    return store(h, tail_base, tail_got, whole, partial)


def solution(mesh):
    in_specs = (
        P(None, "row", "col"),
        P(),
        P("row", "col", None, None, None),
        P("row", "col", None, None),
        P("row", "col"),
    )
    out_specs = P(None, "row", "col")
    return jax.shard_map(
        on_device, mesh=mesh, in_specs=in_specs, out_specs=out_specs, check_vma=False
    )
```

```python
import functools
import math

import jax
import jax.numpy as jnp
from jax import lax
from jax.experimental import pallas as pl
from jax.experimental.pallas import tpu as pltpu
from jax.sharding import PartitionSpec as P

STEP = 0.5
FLOOR = 0.05
VMEM = pl.BlockSpec(memory_space=pltpu.VMEM)
ANY = pl.BlockSpec(memory_space=pl.ANY)
SMEM = pl.BlockSpec(memory_space=pltpu.SMEM)
LIMIT = 12 * 1024 * 1024
F32 = jnp.float32
BF16 = jnp.bfloat16

EXTRA = 8
HEAD = 240
HEAD_PIECES = 1
TAIL_PIECES = 2


def shifted(value, axis, steps):
    count = lax.axis_size(axis)
    leading, last = (max(0, -steps), min(count, count - steps))
    return lax.ppermute(value, axis, [(source, source + steps) for source in range(leading, last)])


def dft_tables(width):
    index = jnp.arange(width, dtype=jnp.int32)
    phase = index[:, None] * index[None, :] % width
    angle = phase.astype(jnp.float32) * (2.0 * math.pi / width)
    scale = 1.0 / math.sqrt(width)
    return (
        (jnp.cos(angle) * scale).astype(jnp.bfloat16),
        (jnp.sin(angle) * scale).astype(jnp.bfloat16),
    )


def call(kernel, outs, arrays, scratch=(), scalars=(), after=()):
    flat, tree = jax.tree.flatten(tuple(arrays))
    out_flat, out_tree = jax.tree.flatten(tuple(outs))
    skip, count = len(after), len(scalars)

    def body(*refs):
        refs = refs[skip:]
        numbers, refs = refs[:count], refs[count:]
        given = jax.tree.unflatten(tree, refs[: len(flat)])
        made = jax.tree.unflatten(out_tree, refs[len(flat) : len(flat) + len(out_flat)])
        kernel(*numbers, *given, *made, *refs[len(flat) + len(out_flat) :])

    results = pl.pallas_call(
        body,
        out_shape=out_flat,
        in_specs=[ANY] * skip + [SMEM] * count + [VMEM] * len(flat),
        out_specs=[VMEM] * len(out_flat),
        scratch_shapes=list(scratch),
        compiler_params=pltpu.CompilerParams(vmem_limit_bytes=LIMIT),
    )(*after, *scalars, *flat)
    return jax.tree.unflatten(out_tree, results)


def split(first, width):
    height, count = (HEAD, HEAD_PIECES) if first == 0 else (width - HEAD, TAIL_PIECES)
    size = height // count
    return [(k, first + k * size, slice(k * size, (k + 1) * size)) for k in range(count)]


def part(half, plane, k, rows):
    if isinstance(half, list):
        return half[k][plane, : rows.stop - rows.start, :]
    return half[plane, rows, :]


def put(half, plane, k, rows, value):
    if isinstance(half, list):
        half[k][plane, : rows.stop - rows.start, :] = value
    else:
        half[plane, rows, :] = value


def indices(rows, width, first):
    shape = (rows.stop - rows.start, width)
    return (
        lax.broadcasted_iota(jnp.int32, shape, 0) + first,
        lax.broadcasted_iota(jnp.int32, shape, 1),
    )


def low(i, place):
    return i + 1 < place[0, :1, :].astype(jnp.int32)


def far(j, place):
    return j + 1 < place[1, :1, :].astype(jnp.int32)


def ways_of(head, rows, width, first):
    i, j = indices(rows, width, first)
    pair = (functools.partial(low, i), functools.partial(far, j))
    return pair if head else pair[::-1]


def absent(place):
    return place[0, :1, :] == 0.0


def prepare_kernel(offset, cos_ref, sin_ref, pupil_ref, bx, bxt, by, byt_head, byt_tail, pupil_out):
    w = cos_ref.shape[0]
    h = HEAD
    cosine = cos_ref[...].astype(F32)
    sine = sin_ref[...].astype(F32)
    oy, ox = offset[0, 0], offset[0, 1]

    def rolled(value, shift, axis):
        return pltpu.roll(value, shift, axis)

    c, s = rolled(cosine, ox, 0).astype(BF16), rolled(sine, ox, 0).astype(BF16)
    bx[:w, :w], bx[:w, w:], bx[w:, :w], bx[w:, w:] = c, s, -s, c
    c, s = rolled(cosine, ox, 1).astype(BF16), rolled(sine, ox, 1).astype(BF16)
    bxt[:w, :w], bxt[:w, w:], bxt[w:, :w], bxt[w:, w:] = c, -s, s, c
    c, s = rolled(cosine, oy, 0).astype(BF16), rolled(sine, oy, 0).astype(BF16)
    by[:w, :w], by[:w, w:], by[w:, :w], by[w:, w:] = c, s, -s, c
    c, s = rolled(cosine, oy, 1).astype(BF16), rolled(sine, oy, 1).astype(BF16)
    for out, cols in ((byt_head, slice(0, h)), (byt_tail, slice(h, w))):
        n = cols.stop - cols.start
        out[:w, :n], out[:w, n:] = c[:, cols], -s[:, cols]
        out[w:, :n], out[w:, n:] = s[:, cols], c[:, cols]
    for plane in range(2):
        pupil_out[plane] = rolled(rolled(pupil_ref[plane], oy, 0), ox, 1)


def dot(a, b):
    return jnp.dot(a, b, preferred_element_type=F32)


def right_product(first, window, pupil, bx, left, half):
    w = bx.shape[0] // 2
    h = half.shape[0] // 2
    for k, row, rows in split(first, w):
        wr, wi = window(k, row, rows)
        across = slice(row, row + rows.stop - rows.start)
        pr, pi = pupil[0, across, :], pupil[1, across, :]
        left[rows, :w] = (wr * pr - wi * pi).astype(BF16)
        left[rows, w:] = (wr * pi + wi * pr).astype(BF16)
    half[:h, :] = dot(left[:h, :], bx[:, :w]).astype(BF16)
    half[h:, :] = dot(left[:h, :], bx[:, w:]).astype(BF16)


def finish(acc, byt_tail, half, amp, live, bxt, left, stacked):
    w = amp.shape[0]
    block = 128
    alive = (live[0, 0] > 0).astype(F32)
    for first in range(0, w, block):
        rows = slice(first, first + block)
        lower = slice(w + first, w + first + block)
        wave_r = acc[rows, :] + dot(byt_tail[rows, :], half[...])
        wave_i = acc[lower, :] + dot(byt_tail[lower, :], half[...])
        power = jnp.maximum(wave_r * wave_r + wave_i * wave_i, FLOOR * FLOOR)
        keep = (1.0 - amp[rows, :] * lax.rsqrt(power)) * alive
        left[rows, :w] = (wave_r * keep).astype(BF16)
        left[rows, w:] = (wave_i * keep).astype(BF16)
    stacked[:w, :] = dot(left[...], bxt[:, :w]).astype(BF16)
    stacked[w:, :] = dot(left[...], bxt[:, w:]).astype(BF16)


def back(first, by, stacked, pupil, out, extra):
    w = stacked.shape[1]
    for k, row, rows in split(first, w):
        size = rows.stop - rows.start
        back_r = dot(by[row : row + size, :], stacked[...])
        back_i = dot(by[w + row : w + row + size, :], stacked[...])
        pr, pi = pupil[0, row : row + size, :], pupil[1, row : row + size, :]
        grad_r = back_r * pr + back_i * pi
        grad_i = back_i * pr - back_r * pi
        if extra is not None:
            grad_r = grad_r + part(extra, 0, k, rows)
            grad_i = grad_i + part(extra, 1, k, rows)
        put(out, 0, k, rows, grad_r)
        put(out, 1, k, rows, grad_i)


def gathered(head, place, tile, one, both, kept):
    def window(k, row, rows):
        first_way, second_way = ways_of(head, rows, kept.shape[2], row)
        a, b = first_way(place), second_way(place)
        values = []
        for plane in range(2):
            near = jnp.where(a, part(one, plane, k, rows), part(tile, plane, k, rows))
            value = jnp.where(b, part(both, plane, k, rows), near)
            kept[plane, rows, :] = value
            values.append(value)
        return values

    return window


def updated(head, place, edge_row, edge_col, kept, own, minus, plus):
    def window(k, row, rows):
        i, j = indices(rows, kept.shape[2], row)
        a, b = low(i, place), far(j, place)
        outside = (a & absent(edge_row)) | (b & absent(edge_col))
        second = b if head else a
        values = []
        for plane in range(2):
            near = jnp.where(second, part(plus, plane, k, rows), part(minus, plane, k, rows))
            value = kept[plane, rows, :] - STEP * (own[plane, rows, :] + near)
            values.append(jnp.where(outside, 0.0, value))
        return values

    return window


def open_first(first, place, tile, one, both, pupil, bx, byt, kept, acc, right_of, left, half):
    right_product(first, gathered(True, place, tile, one, both, kept), pupil, bx, left, half)
    acc[...] = dot(byt[...], half[...])
    right_of[...] = both[-1][:, both[-1].shape[1] - EXTRA :, :]


def close_first(
    first, live, place, tile, one, both, acc, pupil, amp, bx, byt, bxt, by, kept, under, stacked, out, left, half
):
    right_product(first, gathered(False, place, tile, one, both, kept), pupil, bx, left, half)
    finish(acc, byt, half, amp, live, bxt, left, stacked)
    back(0, by, stacked, pupil, out, None)
    under[...] = both[:, both.shape[1] - EXTRA :, :]


def open_second(
    first, place, edge_row, edge_col, kept, own, minus, plus, pupil, bx, byt, acc, left, half
):
    window = updated(True, place, edge_row, edge_col, kept, own, minus, plus)
    right_product(first, window, pupil, bx, left, half)
    acc[...] = dot(byt[...], half[...])


def close_second(
    first, live, place, edge_row, edge_col, kept, own, minus, plus, acc, pupil, amp, bx, byt, bxt, by,
    extra, stacked, out, left, half
):
    window = updated(False, place, edge_row, edge_col, kept, own, minus, plus)
    right_product(first, window, pupil, bx, left, half)
    finish(acc, byt, half, amp, live, bxt, left, stacked)
    back(0, by, stacked, pupil, out, extra)


def rest_first(first, by, stacked, pupil, out):
    back(first, by, stacked, pupil, out, None)


def rest_second(first, by, stacked, pupil, extra, out):
    back(first, by, stacked, pupil, out, extra)


def compose_kernel(first, head, me, target, tile, one, out):
    w = me.shape[2]
    for k, row, rows in split(first, w):
        mask = ways_of(head, rows, w, row)[0](target)
        for plane in range(2):
            value = jnp.where(mask, part(one, plane, k, rows), part(tile, plane, k, rows))
            put(out, plane, k, rows, value)
    end = out[-1] if head else out
    end[:, end.shape[1] - EXTRA :, :] = me[...]


def between_kernel(
    first, head, me, minus, plus, target_minus, target_plus, mine, got_minus, got_plus, to_minus, to_plus, own
):
    w = me.shape[2]
    for k, row, rows in split(first, w):
        ways = ways_of(head, rows, w, row)
        f, f_minus, f_plus = (ways[0](x) for x in (me, minus, plus))
        s, s_minus, s_plus = (ways[1](x) for x in (me, minus, plus))

        def seen(goal):
            return f == goal, ~goal & f_minus, goal & ~f_plus

        minus_m = [a & ~b for a, b in zip(seen(ways[0](target_minus)), (s, s_minus, s_plus))]
        plus_m = [a & b for a, b in zip(seen(ways[0](target_plus)), (s, s_minus, s_plus))]
        _, own_minus, own_plus = seen(f)
        own_minus, own_plus = own_minus & (s == s_minus), own_plus & (s == s_plus)
        for plane in range(2):
            values = [part(x, plane, k, rows) for x in (mine, got_minus, got_plus)]
            for out, masks in ((to_minus, minus_m), (to_plus, plus_m)):
                terms = [jnp.where(m, v, 0.0) for m, v in zip(masks, values)]
                put(out, plane, k, rows, terms[0] + terms[1] + terms[2])
            others = jnp.where(own_minus, values[1], 0.0) + jnp.where(own_plus, values[2], 0.0)
            put(own, plane, k, rows, values[0] + others)


def final_kernel(first, head, me, minus, tile, mine, got, to_plus, base):
    w = me.shape[2]
    for k, row, rows in split(first, w):
        ways = ways_of(head, rows, w, row)
        f, f_minus = ways[0](me), ways[0](minus)
        s, s_minus = ways[1](me), ways[1](minus)
        for plane in range(2):
            own = jnp.where(f, 0.0, part(mine, plane, k, rows))
            other = jnp.where(f_minus, part(got, plane, k, rows), 0.0)
            put(to_plus, plane, k, rows, jnp.where(s, own, 0.0) + jnp.where(s_minus, other, 0.0))
            kept = jnp.where(s, 0.0, own) + jnp.where(s_minus, 0.0, other)
            base[plane, rows, :] = part(tile, plane, k, rows) - STEP * kept


def store(first, base, got, whole, previous=None):
    _, h, w = base.shape
    held = () if previous is None else (previous,)
    got = got if isinstance(got, list) else [got]

    def kernel(base, *refs):
        pieces = refs[: len(got)]
        out, value, sems = refs[-3:]
        copies, row = [], 0
        for k, piece in enumerate(pieces):
            size = piece.shape[1]
            rows = slice(row, row + size)
            value[:, rows, :] = base[:, rows, :] - STEP * piece[...]
            copy = pltpu.make_async_copy(
                value.at[:, pl.ds(row, size), :], out.at[:, pl.ds(first + row, size), :], sems.at[k]
            )
            copy.start()
            copies.append(copy)
            row += size
        for copy in copies:
            copy.wait()

    return pl.pallas_call(
        kernel,
        out_shape=whole,
        in_specs=[VMEM] * (1 + len(got)) + [ANY] * len(held),
        out_specs=ANY,
        scratch_shapes=[pltpu.VMEM((2, h, w), F32), pltpu.SemaphoreType.DMA((len(got),))],
        input_output_aliases={1 + len(got): 0} if held else {},
        compiler_params=pltpu.CompilerParams(vmem_limit_bytes=LIMIT),
    )(base, *got, *held)


def on_device(spectrum, pupil, amplitudes, offsets, counts):
    w = pupil.shape[1]
    h = HEAD
    amp = amplitudes[0, 0, 0]
    offset = offsets[0, 0]

    def block(rows):
        return jax.ShapeDtypeStruct((2, rows, w), F32)

    head_half, tail_half, whole, spot = block(h), block(w - h), block(w), block(EXTRA)
    head_pieces, tail_pieces = (
        [block(rows.stop - rows.start) for _, _, rows in split(first, w)] for first in (0, h)
    )
    me = jnp.broadcast_to((offset[0] + 1).astype(F32)[:, None, None], (2, EXTRA, w))
    head = spectrum[:, :h]
    tail = [spectrum[:, h + rows.start : h + rows.stop] for _, _, rows in split(h, w)]

    def each(values, axis, steps):
        return [shifted(value, axis, steps) for value in values]

    head_below = shifted(head, "row", -1)
    tail_right = each(tail, "col", -1)
    above = shifted(me, "row", 1)
    left_of = shifted(me, "col", 1)

    cosine, sine = dft_tables(w)
    square = jax.ShapeDtypeStruct((2 * w, 2 * w), BF16)
    stack = jax.ShapeDtypeStruct((2 * w, w), BF16)
    narrow = [jax.ShapeDtypeStruct((2 * w, 2 * n), BF16) for n in (h, w - h)]
    bx, bxt, by, byt_head, byt_tail, rolled = call(
        prepare_kernel, [square] * 3 + narrow + [whole], (cosine, sine, pupil), scalars=(offset,)
    )

    (tail_made,) = call(
        functools.partial(compose_kernel, h, False), [block(w - h + EXTRA)], (me, above, tail, tail_right)
    )
    tail_both = shifted(tail_made, "row", -1)
    (head_made,) = call(
        functools.partial(compose_kernel, 0, True),
        [head_pieces[:-1] + [block(head_pieces[-1].shape[1] + EXTRA)]],
        (me, left_of, head, head_below),
        after=(tail_made,),
    )
    head_both = each(head_made, "col", -1)

    total = jax.ShapeDtypeStruct((2 * w, w), F32)
    products = [pltpu.VMEM((2 * n, w), BF16) for n in (h, w - h)]
    left_half, left_whole = pltpu.VMEM((h, 2 * w), BF16), pltpu.VMEM((w, 2 * w), BF16)
    head_kept, acc, right_of = call(
        functools.partial(open_first, 0),
        [head_half, total, spot],
        (me, head, head_below, head_both, rolled, bx, byt_head),
        (left_half, products[0]),
    )
    tail_kept, under, stacked, head_grad = call(
        functools.partial(close_first, h),
        [tail_half, spot, stack, head_half],
        (me, tail, tail_right, tail_both, acc, rolled, amp, bx, byt_tail, bxt, by),
        (left_whole, products[1]),
        scalars=(counts,),
    )

    got_above, got_under = shifted(head_grad, "row", 1), shifted(head_grad, "row", -1)
    (tail_grad,) = call(functools.partial(rest_first, h), [tail_pieces], (by, stacked, rolled))
    got_left, got_right = each(tail_grad, "col", 1), each(tail_grad, "col", -1)
    to_up, to_down, tail_own = call(
        functools.partial(between_kernel, h, False),
        [tail_half] * 3,
        (me, left_of, right_of, above, under, tail_grad, got_left, got_right),
    )
    tail_sums = (tail_own, shifted(to_down, "row", 1), shifted(to_up, "row", -1))
    to_left, to_right, head_own = call(
        functools.partial(between_kernel, 0, True),
        [head_pieces, head_pieces, head_half],
        (me, above, under, left_of, right_of, head_grad, got_above, got_under),
        after=(to_up,),
    )
    head_sums = (head_own, each(to_right, "col", 1), each(to_left, "col", -1))

    (acc,) = call(
        functools.partial(open_second, 0),
        [total],
        (me, under, right_of, head_kept, *head_sums, rolled, bx, byt_head),
        (left_half, products[0]),
    )
    stacked, head_total = call(
        functools.partial(close_second, h),
        [stack, head_half],
        (me, under, right_of, tail_kept, *tail_sums, acc, rolled, amp, bx, byt_tail, bxt, by, head_grad),
        (left_whole, products[1]),
        scalars=(counts,),
    )

    head_above = shifted(head_total, "row", 1)
    (tail_total,) = call(
        functools.partial(rest_second, h), [tail_pieces], (by, stacked, rolled, tail_grad)
    )
    tail_left = each(tail_total, "col", 1)
    tail_down, tail_base = call(
        functools.partial(final_kernel, h, False), [tail_half] * 2, (me, left_of, tail, tail_total, tail_left)
    )
    tail_got = shifted(tail_down, "row", 1)
    head_right, head_base = call(
        functools.partial(final_kernel, 0, True),
        [head_pieces, head_half],
        (me, above, head, head_total, head_above),
        after=(tail_down,),
    )
    head_got = each(head_right, "col", 1)
    partial = store(0, head_base, head_got, whole)
    return store(h, tail_base, tail_got, whole, partial)


def solution(mesh):
    in_specs = (
        P(None, "row", "col"),
        P(),
        P("row", "col", None, None, None),
        P("row", "col", None, None),
        P("row", "col"),
    )
    out_specs = P(None, "row", "col")
    return jax.shard_map(
        on_device, mesh=mesh, in_specs=in_specs, out_specs=out_specs, check_vma=False
    )
```

```python
import functools
import math

import jax
import jax.numpy as jnp
from jax import lax
from jax.experimental import pallas as pl
from jax.experimental.pallas import tpu as pltpu
from jax.sharding import PartitionSpec as P

STEP = 0.5
FLOOR = 0.05
VMEM = pl.BlockSpec(memory_space=pltpu.VMEM)
ANY = pl.BlockSpec(memory_space=pl.ANY)
SMEM = pl.BlockSpec(memory_space=pltpu.SMEM)
LIMIT = 12 * 1024 * 1024
F32 = jnp.float32
BF16 = jnp.bfloat16

EXTRA = 8
BLOCK = 128
PAD = 8


def shifted(value, axis, steps):
    count = lax.axis_size(axis)
    leading, last = (max(0, -steps), min(count, count - steps))
    return lax.ppermute(value, axis, [(source, source + steps) for source in range(leading, last)])


def dft_tables(width):
    index = jnp.arange(width, dtype=jnp.int32)
    phase = index[:, None] * index[None, :] % width
    angle = phase.astype(jnp.float32) * (2.0 * math.pi / width)
    scale = 1.0 / math.sqrt(width)
    return (
        (jnp.cos(angle) * scale).astype(jnp.bfloat16),
        (jnp.sin(angle) * scale).astype(jnp.bfloat16),
    )


def call(kernel, outs, arrays, scratch=(), scalars=(), after=()):
    flat, tree = jax.tree.flatten(tuple(arrays))
    out_flat, out_tree = jax.tree.flatten(tuple(outs))
    skip, count = len(after), len(scalars)

    def body(*refs):
        refs = refs[skip:]
        numbers, refs = refs[:count], refs[count:]
        given = jax.tree.unflatten(tree, refs[: len(flat)])
        made = jax.tree.unflatten(out_tree, refs[len(flat) : len(flat) + len(out_flat)])
        kernel(*numbers, *given, *made, *refs[len(flat) + len(out_flat) :])

    results = pl.pallas_call(
        body,
        out_shape=out_flat,
        in_specs=[ANY] * skip + [SMEM] * count + [VMEM] * len(flat),
        out_specs=[VMEM] * len(out_flat),
        scratch_shapes=list(scratch),
        compiler_params=pltpu.CompilerParams(vmem_limit_bytes=LIMIT),
    )(*after, *scalars, *flat)
    return jax.tree.unflatten(out_tree, results)


def split(first, width):
    return [(first + row, slice(row, row + BLOCK)) for row in range(0, width // 2, BLOCK)]


def place_in(half, rows, width):
    if not isinstance(half, list):
        return half, rows
    height = width // 2 // len(half)
    index = rows.start // height
    return half[index], slice(rows.start - index * height, rows.stop - index * height)


def part(half, plane, rows, width):
    array, inner = place_in(half, rows, width)
    return array[plane, inner, :]


def put(half, plane, rows, value):
    array, inner = place_in(half, rows, value.shape[1])
    array[plane, inner, :] = value


def indices(rows, width, first):
    shape = (rows.stop - rows.start, width)
    return (
        lax.broadcasted_iota(jnp.int32, shape, 0) + first,
        lax.broadcasted_iota(jnp.int32, shape, 1),
    )


def low(i, place):
    return i + 1 < place[0, :1, :].astype(jnp.int32)


def far(j, place):
    return j + 1 < place[1, :1, :].astype(jnp.int32)


def ways_of(head, rows, width, first):
    i, j = indices(rows, width, first)
    pair = (functools.partial(low, i), functools.partial(far, j))
    return pair if head else pair[::-1]


def absent(place):
    return place[0, :1, :] == 0.0


def prepare_kernel(offset, cos_ref, sin_ref, pupil_ref, bx, bxt, by, byt_head, byt_tail, pupil_out):
    w = cos_ref.shape[0]
    h = w // 2
    cosine = cos_ref[...].astype(F32)
    sine = sin_ref[...].astype(F32)
    oy, ox = offset[0, 0], offset[0, 1]

    def rolled(value, shift, axis):
        return pltpu.roll(value, shift, axis)

    c, s = rolled(cosine, ox, 0).astype(BF16), rolled(sine, ox, 0).astype(BF16)
    bx[:w, :w], bx[:w, w:], bx[w:, :w], bx[w:, w:] = c, s, -s, c
    c, s = rolled(cosine, ox, 1).astype(BF16), rolled(sine, ox, 1).astype(BF16)
    bxt[:w, :w], bxt[:w, w:], bxt[w:, :w], bxt[w:, w:] = c, -s, s, c
    c, s = rolled(cosine, oy, 0).astype(BF16), rolled(sine, oy, 0).astype(BF16)
    by[:w, :w], by[:w, w:], by[w:, :w], by[w:, w:] = c, s, -s, c
    c, s = rolled(cosine, oy, 1).astype(BF16), rolled(sine, oy, 1).astype(BF16)
    for out, cols in ((byt_head, slice(0, h)), (byt_tail, slice(h, w))):
        n = cols.stop - cols.start
        out[:w, :n], out[:w, n:] = c[:, cols], -s[:, cols]
        out[w:, :n], out[w:, n:] = s[:, cols], c[:, cols]
    for plane in range(2):
        pupil_out[plane] = rolled(rolled(pupil_ref[plane], oy, 0), ox, 1)


def dot(a, b):
    return jnp.dot(a, b, preferred_element_type=F32)


def right_product(first, window, pupil, bx, left, half):
    w = bx.shape[0] // 2
    h = half.shape[0] // 2
    for row, rows in split(first, w):
        wr, wi = window(row, rows)
        across = slice(row, row + rows.stop - rows.start)
        pr, pi = pupil[0, across, :], pupil[1, across, :]
        left[rows, :w] = (wr * pr - wi * pi).astype(BF16)
        left[rows, w:] = (wr * pi + wi * pr).astype(BF16)
    half[:h, :] = dot(left[:h, :], bx[:, :w]).astype(BF16)
    half[h:, :] = dot(left[:h, :], bx[:, w:]).astype(BF16)


def finish(acc, byt_tail, half, amp, live, bxt, left, stacked):
    w = amp.shape[0]
    block = 128
    alive = (live[0, 0] > 0).astype(F32)
    for first in range(0, w, block):
        rows = slice(first, first + block)
        lower = slice(w + first, w + first + block)
        wave_r = acc[rows, :] + dot(byt_tail[rows, :], half[...])
        wave_i = acc[lower, :] + dot(byt_tail[lower, :], half[...])
        power = jnp.maximum(wave_r * wave_r + wave_i * wave_i, FLOOR * FLOOR)
        keep = (1.0 - amp[rows, :] * lax.rsqrt(power)) * alive
        left[rows, :w] = (wave_r * keep).astype(BF16)
        left[rows, w:] = (wave_i * keep).astype(BF16)
    stacked[:w, :] = dot(left[...], bxt[:, :w]).astype(BF16)
    stacked[w:, :] = dot(left[...], bxt[:, w:]).astype(BF16)


def back(first, by, stacked, pupil, out, extra):
    w = stacked.shape[1]
    for row, rows in split(first, w):
        size = rows.stop - rows.start
        back_r = dot(by[row : row + size, :], stacked[...])
        back_i = dot(by[w + row : w + row + size, :], stacked[...])
        pr, pi = pupil[0, row : row + size, :], pupil[1, row : row + size, :]
        grad_r = back_r * pr + back_i * pi
        grad_i = back_i * pr - back_r * pi
        if extra is not None:
            grad_r = grad_r + part(extra, 0, rows, w)
            grad_i = grad_i + part(extra, 1, rows, w)
        put(out, 0, rows, grad_r)
        put(out, 1, rows, grad_i)


def gathered(head, place, tile, one, both, kept):
    w = kept.shape[2]

    def window(row, rows):
        first_way, second_way = ways_of(head, rows, w, row)
        a, b = first_way(place), second_way(place)
        values = []
        for plane in range(2):
            near = jnp.where(a, part(one, plane, rows, w), part(tile, plane, rows, w))
            value = jnp.where(b, part(both, plane, rows, w), near)
            kept[plane, rows, :] = value
            values.append(value)
        return values

    return window


def updated(head, place, edge_row, edge_col, kept, own, minus, plus):
    w = kept.shape[2]

    def window(row, rows):
        i, j = indices(rows, w, row)
        a, b = low(i, place), far(j, place)
        outside = (a & absent(edge_row)) | (b & absent(edge_col))
        second = b if head else a
        values = []
        for plane in range(2):
            near = jnp.where(second, part(plus, plane, rows, w), part(minus, plane, rows, w))
            value = kept[plane, rows, :] - STEP * (own[plane, rows, :] + near)
            values.append(jnp.where(outside, 0.0, value))
        return values

    return window


def open_first(first, place, tile, one, both, pupil, bx, byt, kept, acc, right_of, left, half):
    right_product(first, gathered(True, place, tile, one, both, kept), pupil, bx, left, half)
    acc[...] = dot(byt[...], half[...])
    right_of[...] = both[-1][:, both[-1].shape[1] - EXTRA :, :]


def close_first(
    first, live, place, tile, one, both, acc, pupil, amp, bx, byt, bxt, by, kept, under, stacked, out, left, half
):
    right_product(first, gathered(False, place, tile, one, both, kept), pupil, bx, left, half)
    finish(acc, byt, half, amp, live, bxt, left, stacked)
    back(0, by, stacked, pupil, out, None)
    under[...] = both[:, both.shape[1] - EXTRA :, :]


def open_second(
    first, place, edge_row, edge_col, kept, own, minus, plus, pupil, bx, byt, acc, left, half
):
    window = updated(True, place, edge_row, edge_col, kept, own, minus, plus)
    right_product(first, window, pupil, bx, left, half)
    acc[...] = dot(byt[...], half[...])


def close_second(
    first, live, place, edge_row, edge_col, kept, own, minus, plus, acc, pupil, amp, bx, byt, bxt, by,
    extra, stacked, out, left, half
):
    window = updated(False, place, edge_row, edge_col, kept, own, minus, plus)
    right_product(first, window, pupil, bx, left, half)
    finish(acc, byt, half, amp, live, bxt, left, stacked)
    back(0, by, stacked, pupil, out, extra)


def rest_first(first, by, stacked, pupil, out):
    back(first, by, stacked, pupil, out, None)


def rest_second(first, by, stacked, pupil, extra, out):
    back(first, by, stacked, pupil, out, extra)


def compose_kernel(first, head, me, target, tile, one, out):
    w = me.shape[2]
    for row, rows in split(first, w):
        mask = ways_of(head, rows, w, row)[0](target)
        for plane in range(2):
            value = jnp.where(mask, part(one, plane, rows, w), part(tile, plane, rows, w))
            put(out, plane, rows, value)
    end = out[-1] if head else out
    end[:, end.shape[1] - EXTRA :, :] = me[...]


def between_kernel(
    first, head, me, minus, plus, target_minus, target_plus, mine, got_minus, got_plus, to_minus, to_plus, own
):
    w = me.shape[2]
    for row, rows in split(first, w):
        ways = ways_of(head, rows, w, row)
        f, f_minus, f_plus = (ways[0](x) for x in (me, minus, plus))
        s, s_minus, s_plus = (ways[1](x) for x in (me, minus, plus))

        def seen(goal):
            return f == goal, ~goal & f_minus, goal & ~f_plus

        minus_m = [a & ~b for a, b in zip(seen(ways[0](target_minus)), (s, s_minus, s_plus))]
        plus_m = [a & b for a, b in zip(seen(ways[0](target_plus)), (s, s_minus, s_plus))]
        _, own_minus, own_plus = seen(f)
        own_minus, own_plus = own_minus & (s == s_minus), own_plus & (s == s_plus)
        for plane in range(2):
            values = [part(x, plane, rows, w) for x in (mine, got_minus, got_plus)]
            for out, masks in ((to_minus, minus_m), (to_plus, plus_m)):
                terms = [jnp.where(m, v, 0.0) for m, v in zip(masks, values)]
                put(out, plane, rows, terms[0] + terms[1] + terms[2])
            others = jnp.where(own_minus, values[1], 0.0) + jnp.where(own_plus, values[2], 0.0)
            put(own, plane, rows, values[0] + others)


def final_kernel(first, head, me, minus, tile, mine, got, to_plus, base):
    w = me.shape[2]
    for row, rows in split(first, w):
        ways = ways_of(head, rows, w, row)
        f, f_minus = ways[0](me), ways[0](minus)
        s, s_minus = ways[1](me), ways[1](minus)
        for plane in range(2):
            own = jnp.where(f, 0.0, part(mine, plane, rows, w))
            other = jnp.where(f_minus, part(got, plane, rows, w), 0.0)
            put(to_plus, plane, rows, jnp.where(s, own, 0.0) + jnp.where(s_minus, other, 0.0))
            kept = jnp.where(s, 0.0, own) + jnp.where(s_minus, 0.0, other)
            base[plane, rows, :] = part(tile, plane, rows, w) - STEP * kept


def store(first, base, got, whole, previous=None):
    _, h, w = base.shape
    held = () if previous is None else (previous,)
    got = got if isinstance(got, list) else [got]

    def kernel(base, *refs):
        pieces = refs[: len(got)]
        out, value, sems = refs[-3:]
        copies, row = [], 0
        for k, piece in enumerate(pieces):
            size = min(piece.shape[1], h - row)
            rows = slice(row, row + size)
            value[:, rows, :] = base[:, rows, :] - STEP * piece[:, :size, :]
            copy = pltpu.make_async_copy(
                value.at[:, pl.ds(row, size), :], out.at[:, pl.ds(first + row, size), :], sems.at[k]
            )
            copy.start()
            copies.append(copy)
            row += size
        for copy in copies:
            copy.wait()

    return pl.pallas_call(
        kernel,
        out_shape=whole,
        in_specs=[VMEM] * (1 + len(got)) + [ANY] * len(held),
        out_specs=ANY,
        scratch_shapes=[pltpu.VMEM((2, h, w), F32), pltpu.SemaphoreType.DMA((len(got),))],
        input_output_aliases={1 + len(got): 0} if held else {},
        compiler_params=pltpu.CompilerParams(vmem_limit_bytes=LIMIT),
    )(base, *got, *held)


def on_device(spectrum, pupil, amplitudes, offsets, counts):
    w = pupil.shape[1]
    h = w // 2
    amp = amplitudes[0, 0, 0]
    offset = offsets[0, 0]

    def block(rows):
        return jax.ShapeDtypeStruct((2, rows, w), F32)

    half, whole, spot = block(h), block(w), block(EXTRA)
    pieces = [block(h // 2)] * 2
    me = jnp.broadcast_to((offset[0] + 1).astype(F32)[:, None, None], (2, EXTRA, w))
    head = spectrum[:, :h]
    tail = [spectrum[:, h : h + h // 2], spectrum[:, h + h // 2 :]]

    def each(values, axis, steps):
        return [shifted(value, axis, steps) for value in values]

    head_below = shifted(head, "row", -1)
    tail_right = each(tail, "col", -1)
    above = shifted(me, "row", 1)
    left_of = shifted(me, "col", 1)

    cosine, sine = dft_tables(w)
    square = jax.ShapeDtypeStruct((2 * w, 2 * w), BF16)
    stack = jax.ShapeDtypeStruct((2 * w, w), BF16)
    bx, bxt, by, byt_head, byt_tail, rolled = call(
        prepare_kernel, [square] * 3 + [stack] * 2 + [whole], (cosine, sine, pupil), scalars=(offset,)
    )

    (tail_made,) = call(
        functools.partial(compose_kernel, h, False), [block(h + EXTRA)], (me, above, tail, tail_right)
    )
    tail_both = shifted(tail_made, "row", -1)
    (head_made,) = call(
        functools.partial(compose_kernel, 0, True),
        [[pieces[0], block(h // 2 + EXTRA)]],
        (me, left_of, head, head_below),
        after=(tail_made,),
    )
    head_both = each(head_made, "col", -1)

    total = jax.ShapeDtypeStruct((2 * w, w), F32)
    products = pltpu.VMEM((w, w), BF16)
    left_half, left_whole = pltpu.VMEM((h, 2 * w), BF16), pltpu.VMEM((w, 2 * w), BF16)
    head_kept, acc, right_of = call(
        functools.partial(open_first, 0),
        [half, total, spot],
        (me, head, head_below, head_both, rolled, bx, byt_head),
        (left_half, products),
    )
    tail_kept, under, stacked, head_grad = call(
        functools.partial(close_first, h),
        [half, spot, stack, block(h + PAD)],
        (me, tail, tail_right, tail_both, acc, rolled, amp, bx, byt_tail, bxt, by),
        (left_whole, products),
        scalars=(counts,),
    )

    got_above, got_under = shifted(head_grad, "row", 1), shifted(head_grad, "row", -1)
    (tail_grad,) = call(functools.partial(rest_first, h), [[half]], (by, stacked, rolled))
    got_left, got_right = each(tail_grad, "col", 1), each(tail_grad, "col", -1)
    to_up, to_down, tail_own = call(
        functools.partial(between_kernel, h, False),
        [block(h + PAD)] * 2 + [half],
        (me, left_of, right_of, above, under, tail_grad, got_left, got_right),
    )
    tail_sums = (tail_own, shifted(to_down, "row", 1), shifted(to_up, "row", -1))
    to_left, to_right, head_own = call(
        functools.partial(between_kernel, 0, True),
        [[half], [half], half],
        (me, above, under, left_of, right_of, head_grad, got_above, got_under),
        after=(to_up,),
    )
    head_sums = (head_own, each(to_right, "col", 1), each(to_left, "col", -1))

    (acc,) = call(
        functools.partial(open_second, 0),
        [total],
        (me, under, right_of, head_kept, *head_sums, rolled, bx, byt_head),
        (left_half, products),
    )
    stacked, head_total = call(
        functools.partial(close_second, h),
        [stack, half],
        (me, under, right_of, tail_kept, *tail_sums, acc, rolled, amp, bx, byt_tail, bxt, by, head_grad),
        (left_whole, products),
        scalars=(counts,),
    )

    head_above = shifted(head_total, "row", 1)
    (tail_total,) = call(
        functools.partial(rest_second, h), [pieces], (by, stacked, rolled, tail_grad)
    )
    tail_left = each(tail_total, "col", 1)
    tail_down, tail_base = call(
        functools.partial(final_kernel, h, False), [half, half], (me, left_of, tail, tail_total, tail_left)
    )
    tail_got = shifted(tail_down, "row", 1)
    head_right, head_base = call(
        functools.partial(final_kernel, 0, True),
        [pieces, half],
        (me, above, head, head_total, head_above),
        after=(tail_down,),
    )
    head_got = each(head_right, "col", 1)
    partial = store(0, head_base, head_got, whole)
    return store(h, tail_base, tail_got, whole, partial)


def solution(mesh):
    in_specs = (
        P(None, "row", "col"),
        P(),
        P("row", "col", None, None, None),
        P("row", "col", None, None),
        P("row", "col"),
    )
    out_specs = P(None, "row", "col")
    return jax.shard_map(
        on_device, mesh=mesh, in_specs=in_specs, out_specs=out_specs, check_vma=False
    )
```

```python
import functools
import math

import jax
import jax.numpy as jnp
from jax import lax
from jax.experimental import pallas as pl
from jax.experimental.pallas import tpu as pltpu
from jax.sharding import PartitionSpec as P

STEP = 0.5
FLOOR = 0.05
VMEM = pl.BlockSpec(memory_space=pltpu.VMEM)
ANY = pl.BlockSpec(memory_space=pl.ANY)
SMEM = pl.BlockSpec(memory_space=pltpu.SMEM)
LIMIT = 12 * 1024 * 1024
F32 = jnp.float32
BF16 = jnp.bfloat16

EXTRA = 8
BLOCK = 128
PAD = 8


def shifted(value, axis, steps):
    count = lax.axis_size(axis)
    leading, last = (max(0, -steps), min(count, count - steps))
    return lax.ppermute(value, axis, [(source, source + steps) for source in range(leading, last)])


def dft_tables(width):
    index = jnp.arange(width, dtype=jnp.int32)
    phase = index[:, None] * index[None, :] % width
    angle = phase.astype(jnp.float32) * (2.0 * math.pi / width)
    scale = 1.0 / math.sqrt(width)
    return (
        (jnp.cos(angle) * scale).astype(jnp.bfloat16),
        (jnp.sin(angle) * scale).astype(jnp.bfloat16),
    )


def call(kernel, outs, arrays, scratch=(), scalars=(), after=()):
    flat, tree = jax.tree.flatten(tuple(arrays))
    out_flat, out_tree = jax.tree.flatten(tuple(outs))
    skip, count = len(after), len(scalars)

    def body(*refs):
        refs = refs[skip:]
        numbers, refs = refs[:count], refs[count:]
        given = jax.tree.unflatten(tree, refs[: len(flat)])
        made = jax.tree.unflatten(out_tree, refs[len(flat) : len(flat) + len(out_flat)])
        kernel(*numbers, *given, *made, *refs[len(flat) + len(out_flat) :])

    results = pl.pallas_call(
        body,
        out_shape=out_flat,
        in_specs=[ANY] * skip + [SMEM] * count + [VMEM] * len(flat),
        out_specs=[VMEM] * len(out_flat),
        scratch_shapes=list(scratch),
        compiler_params=pltpu.CompilerParams(vmem_limit_bytes=LIMIT),
    )(*after, *scalars, *flat)
    return jax.tree.unflatten(out_tree, results)


def split(first, width):
    return [(first + row, slice(row, row + BLOCK)) for row in range(0, width // 2, BLOCK)]


def place_in(half, rows, width):
    if not isinstance(half, list):
        return half, rows
    height = width // 2 // len(half)
    index = rows.start // height
    return half[index], slice(rows.start - index * height, rows.stop - index * height)


def part(half, plane, rows, width):
    array, inner = place_in(half, rows, width)
    return array[plane, inner, :]


def put(half, plane, rows, value):
    array, inner = place_in(half, rows, value.shape[1])
    array[plane, inner, :] = value


def indices(rows, width, first):
    shape = (rows.stop - rows.start, width)
    return (
        lax.broadcasted_iota(jnp.int32, shape, 0) + first,
        lax.broadcasted_iota(jnp.int32, shape, 1),
    )


def low(i, place):
    return i + 1 < place[0, :1, :].astype(jnp.int32)


def far(j, place):
    return j + 1 < place[1, :1, :].astype(jnp.int32)


def ways_of(head, rows, width, first):
    i, j = indices(rows, width, first)
    pair = (functools.partial(low, i), functools.partial(far, j))
    return pair if head else pair[::-1]


def absent(place):
    return place[0, :1, :] == 0.0


def prepare_kernel(offset, cos_ref, sin_ref, pupil_ref, bx, bxt, by, byt_head, byt_tail, pupil_out):
    w = cos_ref.shape[0]
    h = w // 2
    cosine = cos_ref[...].astype(F32)
    sine = sin_ref[...].astype(F32)
    oy, ox = offset[0, 0], offset[0, 1]

    def rolled(value, shift, axis):
        return pltpu.roll(value, shift, axis)

    c, s = rolled(cosine, ox, 0).astype(BF16), rolled(sine, ox, 0).astype(BF16)
    bx[:w, :w], bx[:w, w:], bx[w:, :w], bx[w:, w:] = c, s, -s, c
    c, s = rolled(cosine, ox, 1).astype(BF16), rolled(sine, ox, 1).astype(BF16)
    bxt[:w, :w], bxt[:w, w:], bxt[w:, :w], bxt[w:, w:] = c, -s, s, c
    c, s = rolled(cosine, oy, 0).astype(BF16), rolled(sine, oy, 0).astype(BF16)
    by[:w, :w], by[:w, w:], by[w:, :w], by[w:, w:] = c, s, -s, c
    c, s = rolled(cosine, oy, 1).astype(BF16), rolled(sine, oy, 1).astype(BF16)
    for out, cols in ((byt_head, slice(0, h)), (byt_tail, slice(h, w))):
        n = cols.stop - cols.start
        out[:w, :n], out[:w, n:] = c[:, cols], -s[:, cols]
        out[w:, :n], out[w:, n:] = s[:, cols], c[:, cols]
    for plane in range(2):
        pupil_out[plane] = rolled(rolled(pupil_ref[plane], oy, 0), ox, 1)


def dot(a, b):
    return jnp.dot(a, b, preferred_element_type=F32)


def right_product(first, window, pupil, bx, left, half):
    w = bx.shape[0] // 2
    h = half.shape[0] // 2
    for row, rows in split(first, w):
        wr, wi = window(row, rows)
        across = slice(row, row + rows.stop - rows.start)
        pr, pi = pupil[0, across, :], pupil[1, across, :]
        left[rows, :w] = (wr * pr - wi * pi).astype(BF16)
        left[rows, w:] = (wr * pi + wi * pr).astype(BF16)
    half[:h, :] = dot(left[:h, :], bx[:, :w]).astype(BF16)
    half[h:, :] = dot(left[:h, :], bx[:, w:]).astype(BF16)


def finish(acc, byt_tail, half, amp, live, bxt, left, stacked):
    w = amp.shape[0]
    block = 256
    alive = (live[0, 0] > 0).astype(F32)
    for first in range(0, w, block):
        rows = slice(first, first + block)
        lower = slice(w + first, w + first + block)
        wave_r = acc[rows, :] + dot(byt_tail[rows, :], half[...])
        wave_i = acc[lower, :] + dot(byt_tail[lower, :], half[...])
        power = jnp.maximum(wave_r * wave_r + wave_i * wave_i, FLOOR * FLOOR)
        keep = (1.0 - amp[rows, :] * lax.rsqrt(power)) * alive
        left[rows, :w] = (wave_r * keep).astype(BF16)
        left[rows, w:] = (wave_i * keep).astype(BF16)
    stacked[:w, :] = dot(left[...], bxt[:, :w]).astype(BF16)
    stacked[w:, :] = dot(left[...], bxt[:, w:]).astype(BF16)


def back(first, by, stacked, pupil, out, extra):
    w = stacked.shape[1]
    h = w // 2
    back_r = dot(by[first : first + h, :], stacked[...])
    back_i = dot(by[w + first : w + first + h, :], stacked[...])
    for row, rows in split(first, w):
        across = slice(row, row + rows.stop - rows.start)
        pr, pi = pupil[0, across, :], pupil[1, across, :]
        br, bi = back_r[rows, :], back_i[rows, :]
        grad_r = br * pr + bi * pi
        grad_i = bi * pr - br * pi
        if extra is not None:
            grad_r = grad_r + part(extra, 0, rows, w)
            grad_i = grad_i + part(extra, 1, rows, w)
        put(out, 0, rows, grad_r)
        put(out, 1, rows, grad_i)


def gathered(head, place, tile, one, both, kept):
    w = kept.shape[2]

    def window(row, rows):
        first_way, second_way = ways_of(head, rows, w, row)
        a, b = first_way(place), second_way(place)
        values = []
        for plane in range(2):
            near = jnp.where(a, part(one, plane, rows, w), part(tile, plane, rows, w))
            value = jnp.where(b, part(both, plane, rows, w), near)
            kept[plane, rows, :] = value
            values.append(value)
        return values

    return window


def updated(head, place, edge_row, edge_col, kept, own, minus, plus):
    w = kept.shape[2]

    def window(row, rows):
        i, j = indices(rows, w, row)
        a, b = low(i, place), far(j, place)
        outside = (a & absent(edge_row)) | (b & absent(edge_col))
        second = b if head else a
        values = []
        for plane in range(2):
            near = jnp.where(second, part(plus, plane, rows, w), part(minus, plane, rows, w))
            value = kept[plane, rows, :] - STEP * (own[plane, rows, :] + near)
            values.append(jnp.where(outside, 0.0, value))
        return values

    return window


def open_first(first, place, tile, one, both, pupil, bx, byt, kept, acc, right_of, left, half):
    right_product(first, gathered(True, place, tile, one, both, kept), pupil, bx, left, half)
    acc[...] = dot(byt[...], half[...])
    right_of[...] = both[-1][:, both[-1].shape[1] - EXTRA :, :]


def close_first(
    first, live, place, tile, one, both, acc, pupil, amp, bx, byt, bxt, by, kept, under, stacked, out, left, half
):
    right_product(first, gathered(False, place, tile, one, both, kept), pupil, bx, left, half)
    finish(acc, byt, half, amp, live, bxt, left, stacked)
    back(0, by, stacked, pupil, out, None)
    under[...] = both[:, both.shape[1] - EXTRA :, :]


def open_second(
    first, place, edge_row, edge_col, kept, own, minus, plus, pupil, bx, byt, acc, left, half
):
    window = updated(True, place, edge_row, edge_col, kept, own, minus, plus)
    right_product(first, window, pupil, bx, left, half)
    acc[...] = dot(byt[...], half[...])


def close_second(
    first, live, place, edge_row, edge_col, kept, own, minus, plus, acc, pupil, amp, bx, byt, bxt, by,
    extra, stacked, out, left, half
):
    window = updated(False, place, edge_row, edge_col, kept, own, minus, plus)
    right_product(first, window, pupil, bx, left, half)
    finish(acc, byt, half, amp, live, bxt, left, stacked)
    back(0, by, stacked, pupil, out, extra)


def rest_first(first, by, stacked, pupil, out):
    back(first, by, stacked, pupil, out, None)


def rest_second(first, by, stacked, pupil, extra, out):
    back(first, by, stacked, pupil, out, extra)


def compose_kernel(first, head, me, target, tile, one, out):
    w = me.shape[2]
    for row, rows in split(first, w):
        mask = ways_of(head, rows, w, row)[0](target)
        for plane in range(2):
            value = jnp.where(mask, part(one, plane, rows, w), part(tile, plane, rows, w))
            put(out, plane, rows, value)
    end = out[-1] if head else out
    end[:, end.shape[1] - EXTRA :, :] = me[...]


def between_kernel(
    first, head, me, minus, plus, target_minus, target_plus, mine, got_minus, got_plus, to_minus, to_plus
):
    w = me.shape[2]
    for row, rows in split(first, w):
        ways = ways_of(head, rows, w, row)
        f, f_minus, f_plus = (ways[0](x) for x in (me, minus, plus))
        s, s_minus, s_plus = (ways[1](x) for x in (me, minus, plus))

        def seen(goal):
            return f == goal, ~goal & f_minus, goal & ~f_plus

        minus_m = [a & ~b for a, b in zip(seen(ways[0](target_minus)), (s, s_minus, s_plus))]
        plus_m = [a & b for a, b in zip(seen(ways[0](target_plus)), (s, s_minus, s_plus))]
        for plane in range(2):
            values = [part(x, plane, rows, w) for x in (mine, got_minus, got_plus)]
            for out, masks in ((to_minus, minus_m), (to_plus, plus_m)):
                terms = [jnp.where(m, v, 0.0) for m, v in zip(masks, values)]
                put(out, plane, rows, terms[0] + terms[1] + terms[2])


def own_kernel(first, head, me, minus, plus, mine, got_minus, got_plus, own):
    w = me.shape[2]
    for row, rows in split(first, w):
        ways = ways_of(head, rows, w, row)
        f, f_minus, f_plus = (ways[0](x) for x in (me, minus, plus))
        s, s_minus, s_plus = (ways[1](x) for x in (me, minus, plus))
        own_minus, own_plus = ~f & f_minus & (s == s_minus), f & ~f_plus & (s == s_plus)
        for plane in range(2):
            values = [part(x, plane, rows, w) for x in (mine, got_minus, got_plus)]
            others = jnp.where(own_minus, values[1], 0.0) + jnp.where(own_plus, values[2], 0.0)
            put(own, plane, rows, values[0] + others)


def final_kernel(first, head, me, minus, tile, mine, got, to_plus, base):
    w = me.shape[2]
    for row, rows in split(first, w):
        ways = ways_of(head, rows, w, row)
        f, f_minus = ways[0](me), ways[0](minus)
        s, s_minus = ways[1](me), ways[1](minus)
        for plane in range(2):
            own = jnp.where(f, 0.0, part(mine, plane, rows, w))
            other = jnp.where(f_minus, part(got, plane, rows, w), 0.0)
            put(to_plus, plane, rows, jnp.where(s, own, 0.0) + jnp.where(s_minus, other, 0.0))
            kept = jnp.where(s, 0.0, own) + jnp.where(s_minus, 0.0, other)
            base[plane, rows, :] = part(tile, plane, rows, w) - STEP * kept


def store(first, base, got, whole, previous=None):
    _, h, w = base.shape
    held = () if previous is None else (previous,)
    got = got if isinstance(got, list) else [got]

    def kernel(base, *refs):
        pieces = refs[: len(got)]
        out, value, sems = refs[-3:]
        copies, row = [], 0
        for k, piece in enumerate(pieces):
            size = min(piece.shape[1], h - row)
            rows = slice(row, row + size)
            value[:, rows, :] = base[:, rows, :] - STEP * piece[:, :size, :]
            copy = pltpu.make_async_copy(
                value.at[:, pl.ds(row, size), :], out.at[:, pl.ds(first + row, size), :], sems.at[k]
            )
            copy.start()
            copies.append(copy)
            row += size
        for copy in copies:
            copy.wait()

    return pl.pallas_call(
        kernel,
        out_shape=whole,
        in_specs=[VMEM] * (1 + len(got)) + [ANY] * len(held),
        out_specs=ANY,
        scratch_shapes=[pltpu.VMEM((2, h, w), F32), pltpu.SemaphoreType.DMA((len(got),))],
        input_output_aliases={1 + len(got): 0} if held else {},
        compiler_params=pltpu.CompilerParams(vmem_limit_bytes=LIMIT),
    )(base, *got, *held)


def on_device(spectrum, pupil, amplitudes, offsets, counts):
    w = pupil.shape[1]
    h = w // 2
    amp = amplitudes[0, 0, 0]
    offset = offsets[0, 0]

    def block(rows):
        return jax.ShapeDtypeStruct((2, rows, w), F32)

    half, whole, spot = block(h), block(w), block(EXTRA)
    pieces = [block(h // 2)] * 2
    me = jnp.broadcast_to((offset[0] + 1).astype(F32)[:, None, None], (2, EXTRA, w))
    head = spectrum[:, :h]
    tail = [spectrum[:, h : h + h // 2], spectrum[:, h + h // 2 :]]

    def each(values, axis, steps):
        return [shifted(value, axis, steps) for value in values]

    head_below = shifted(head, "row", -1)
    tail_right = each(tail, "col", -1)
    above = shifted(me, "row", 1)
    left_of = shifted(me, "col", 1)

    cosine, sine = dft_tables(w)
    square = jax.ShapeDtypeStruct((2 * w, 2 * w), BF16)
    stack = jax.ShapeDtypeStruct((2 * w, w), BF16)
    bx, bxt, by, byt_head, byt_tail, rolled = call(
        prepare_kernel, [square] * 3 + [stack] * 2 + [whole], (cosine, sine, pupil), scalars=(offset,)
    )

    (tail_made,) = call(
        functools.partial(compose_kernel, h, False), [block(h + EXTRA)], (me, above, tail, tail_right)
    )
    tail_both = shifted(tail_made, "row", -1)
    (head_made,) = call(
        functools.partial(compose_kernel, 0, True),
        [[pieces[0], block(h // 2 + EXTRA)]],
        (me, left_of, head, head_below),
        after=(tail_made,),
    )
    head_both = each(head_made, "col", -1)

    total = jax.ShapeDtypeStruct((2 * w, w), F32)
    products = pltpu.VMEM((w, w), BF16)
    left_half, left_whole = pltpu.VMEM((h, 2 * w), BF16), pltpu.VMEM((w, 2 * w), BF16)
    head_kept, acc, right_of = call(
        functools.partial(open_first, 0),
        [half, total, spot],
        (me, head, head_below, head_both, rolled, bx, byt_head),
        (left_half, products),
    )
    tail_kept, under, stacked, head_grad = call(
        functools.partial(close_first, h),
        [half, spot, stack, block(h + PAD)],
        (me, tail, tail_right, tail_both, acc, rolled, amp, bx, byt_tail, bxt, by),
        (left_whole, products),
        scalars=(counts,),
    )

    got_above, got_under = shifted(head_grad, "row", 1), shifted(head_grad, "row", -1)
    (tail_grad,) = call(functools.partial(rest_first, h), [[half]], (by, stacked, rolled))
    got_left, got_right = each(tail_grad, "col", 1), each(tail_grad, "col", -1)
    to_up, to_down = call(
        functools.partial(between_kernel, h, False),
        [block(h + PAD), block(h + PAD)],
        (me, left_of, right_of, above, under, tail_grad, got_left, got_right),
    )
    (tail_own,) = call(
        functools.partial(own_kernel, h, False),
        [half],
        (me, left_of, right_of, tail_grad, got_left, got_right),
        after=(to_up,),
    )
    tail_sums = (tail_own, shifted(to_down, "row", 1), shifted(to_up, "row", -1))
    to_left, to_right = call(
        functools.partial(between_kernel, 0, True),
        [[half], [half]],
        (me, above, under, left_of, right_of, head_grad, got_above, got_under),
        after=(to_up,),
    )
    (head_own,) = call(
        functools.partial(own_kernel, 0, True),
        [half],
        (me, above, under, head_grad, got_above, got_under),
        after=(to_left[0],),
    )
    head_sums = (head_own, each(to_right, "col", 1), each(to_left, "col", -1))

    (acc,) = call(
        functools.partial(open_second, 0),
        [total],
        (me, under, right_of, head_kept, *head_sums, rolled, bx, byt_head),
        (left_half, products),
    )
    stacked, head_total = call(
        functools.partial(close_second, h),
        [stack, half],
        (me, under, right_of, tail_kept, *tail_sums, acc, rolled, amp, bx, byt_tail, bxt, by, head_grad),
        (left_whole, products),
        scalars=(counts,),
    )

    head_above = shifted(head_total, "row", 1)
    (tail_total,) = call(
        functools.partial(rest_second, h), [pieces], (by, stacked, rolled, tail_grad)
    )
    tail_left = each(tail_total, "col", 1)
    tail_down, tail_base = call(
        functools.partial(final_kernel, h, False), [half, half], (me, left_of, tail, tail_total, tail_left)
    )
    tail_got = shifted(tail_down, "row", 1)
    head_right, head_base = call(
        functools.partial(final_kernel, 0, True),
        [pieces, half],
        (me, above, head, head_total, head_above),
        after=(tail_down,),
    )
    head_got = each(head_right, "col", 1)
    partial = store(0, head_base, head_got, whole)
    return store(h, tail_base, tail_got, whole, partial)


def solution(mesh):
    in_specs = (
        P(None, "row", "col"),
        P(),
        P("row", "col", None, None, None),
        P("row", "col", None, None),
        P("row", "col"),
    )
    out_specs = P(None, "row", "col")
    return jax.shard_map(
        on_device, mesh=mesh, in_specs=in_specs, out_specs=out_specs, check_vma=False
    )
```

```python
import functools
import math

import jax
import jax.numpy as jnp
from jax import lax
from jax.experimental import pallas as pl
from jax.experimental.pallas import tpu as pltpu
from jax.sharding import PartitionSpec as P

STEP = 0.5
FLOOR = 0.05
VMEM = pl.BlockSpec(memory_space=pltpu.VMEM)
ANY = pl.BlockSpec(memory_space=pl.ANY)
SMEM = pl.BlockSpec(memory_space=pltpu.SMEM)
LIMIT = 12 * 1024 * 1024
F32 = jnp.float32
BF16 = jnp.bfloat16

EXTRA = 8
BLOCK = 128
ODD = 1024
PAD = 8


def shifted(value, axis, steps):
    count = lax.axis_size(axis)
    leading, last = (max(0, -steps), min(count, count - steps))
    return lax.ppermute(value, axis, [(source, source + steps) for source in range(leading, last)])


def swapped(value, axis, odd):
    lower = range(1 if odd else 0, lax.axis_size(axis) - 1, 2)
    return lax.ppermute(value, axis, [(a, a + 1) for a in lower] + [(a + 1, a) for a in lower])


def dft_tables(width):
    index = jnp.arange(width, dtype=jnp.int32)
    phase = index[:, None] * index[None, :] % width
    angle = phase.astype(jnp.float32) * (2.0 * math.pi / width)
    scale = 1.0 / math.sqrt(width)
    return (
        (jnp.cos(angle) * scale).astype(jnp.bfloat16),
        (jnp.sin(angle) * scale).astype(jnp.bfloat16),
    )


def call(kernel, outs, arrays, scratch=(), scalars=(), after=()):
    flat, tree = jax.tree.flatten(tuple(arrays))
    out_flat, out_tree = jax.tree.flatten(tuple(outs))
    skip, count = len(after), len(scalars)

    def body(*refs):
        refs = refs[skip:]
        numbers, refs = refs[:count], refs[count:]
        given = jax.tree.unflatten(tree, refs[: len(flat)])
        made = jax.tree.unflatten(out_tree, refs[len(flat) : len(flat) + len(out_flat)])
        kernel(*numbers, *given, *made, *refs[len(flat) + len(out_flat) :])

    results = pl.pallas_call(
        body,
        out_shape=out_flat,
        in_specs=[ANY] * skip + [SMEM] * count + [VMEM] * len(flat),
        out_specs=[VMEM] * len(out_flat),
        scratch_shapes=list(scratch),
        compiler_params=pltpu.CompilerParams(vmem_limit_bytes=LIMIT),
    )(*after, *scalars, *flat)
    return jax.tree.unflatten(out_tree, results)


def split(first, width):
    return [(first + row, slice(row, row + BLOCK)) for row in range(0, width // 2, BLOCK)]


def place_in(half, rows, width):
    if not isinstance(half, list):
        return half, rows
    height = width // 2 // len(half)
    index = rows.start // height
    return half[index], slice(rows.start - index * height, rows.stop - index * height)


def part(half, plane, rows, width):
    array, inner = place_in(half, rows, width)
    return array[plane, inner, :]


def put(half, plane, rows, value):
    array, inner = place_in(half, rows, value.shape[1])
    array[plane, inner, :] = value


def indices(rows, width, first):
    shape = (rows.stop - rows.start, width)
    return (
        lax.broadcasted_iota(jnp.int32, shape, 0) + first,
        lax.broadcasted_iota(jnp.int32, shape, 1),
    )


def low(i, place):
    return i + 1 < (place[0, :1, :].astype(jnp.int32) & (ODD - 1))


def far(j, place):
    return j + 1 < place[1, :1, :].astype(jnp.int32)


def ways_of(head, rows, width, first):
    i, j = indices(rows, width, first)
    pair = (functools.partial(low, i), functools.partial(far, j))
    return pair if head else pair[::-1]


def odd_row(place):
    return place[0, :1, :] >= ODD


def absent(place):
    return place[0, :1, :] == 0.0


def prepare_kernel(offset, cos_ref, sin_ref, pupil_ref, bx, bxt, by, byt_head, byt_tail, pupil_out):
    w = cos_ref.shape[0]
    h = w // 2
    cosine = cos_ref[...].astype(F32)
    sine = sin_ref[...].astype(F32)
    oy, ox = offset[0, 0], offset[0, 1]

    def rolled(value, shift, axis):
        return pltpu.roll(value, shift, axis)

    c, s = rolled(cosine, ox, 0).astype(BF16), rolled(sine, ox, 0).astype(BF16)
    bx[:w, :w], bx[:w, w:], bx[w:, :w], bx[w:, w:] = c, s, -s, c
    c, s = rolled(cosine, ox, 1).astype(BF16), rolled(sine, ox, 1).astype(BF16)
    bxt[:w, :w], bxt[:w, w:], bxt[w:, :w], bxt[w:, w:] = c, -s, s, c
    c, s = rolled(cosine, oy, 0).astype(BF16), rolled(sine, oy, 0).astype(BF16)
    by[:w, :w], by[:w, w:], by[w:, :w], by[w:, w:] = c, s, -s, c
    c, s = rolled(cosine, oy, 1).astype(BF16), rolled(sine, oy, 1).astype(BF16)
    for out, cols in ((byt_head, slice(0, h)), (byt_tail, slice(h, w))):
        n = cols.stop - cols.start
        out[:w, :n], out[:w, n:] = c[:, cols], -s[:, cols]
        out[w:, :n], out[w:, n:] = s[:, cols], c[:, cols]
    for plane in range(2):
        pupil_out[plane] = rolled(rolled(pupil_ref[plane], oy, 0), ox, 1)


def dot(a, b):
    return jnp.dot(a, b, preferred_element_type=F32)


def right_product(first, window, pupil, bx, left, half):
    w = bx.shape[0] // 2
    h = half.shape[0] // 2
    for row, rows in split(first, w):
        wr, wi = window(row, rows)
        across = slice(row, row + rows.stop - rows.start)
        pr, pi = pupil[0, across, :], pupil[1, across, :]
        left[rows, :w] = (wr * pr - wi * pi).astype(BF16)
        left[rows, w:] = (wr * pi + wi * pr).astype(BF16)
    half[:h, :] = dot(left[:h, :], bx[:, :w]).astype(BF16)
    half[h:, :] = dot(left[:h, :], bx[:, w:]).astype(BF16)


def finish(acc, byt_tail, half, amp, live, bxt, left, stacked):
    w = amp.shape[0]
    block = 256
    alive = (live[0, 0] > 0).astype(F32)
    for first in range(0, w, block):
        rows = slice(first, first + block)
        lower = slice(w + first, w + first + block)
        wave_r = acc[rows, :] + dot(byt_tail[rows, :], half[...])
        wave_i = acc[lower, :] + dot(byt_tail[lower, :], half[...])
        power = jnp.maximum(wave_r * wave_r + wave_i * wave_i, FLOOR * FLOOR)
        keep = (1.0 - amp[rows, :] * lax.rsqrt(power)) * alive
        left[rows, :w] = (wave_r * keep).astype(BF16)
        left[rows, w:] = (wave_i * keep).astype(BF16)
    stacked[:w, :] = dot(left[...], bxt[:, :w]).astype(BF16)
    stacked[w:, :] = dot(left[...], bxt[:, w:]).astype(BF16)


def back(first, by, stacked, pupil, out, extra):
    w = stacked.shape[1]
    h = w // 2
    back_r = dot(by[first : first + h, :], stacked[...])
    back_i = dot(by[w + first : w + first + h, :], stacked[...])
    for row, rows in split(first, w):
        across = slice(row, row + rows.stop - rows.start)
        pr, pi = pupil[0, across, :], pupil[1, across, :]
        br, bi = back_r[rows, :], back_i[rows, :]
        grad_r = br * pr + bi * pi
        grad_i = bi * pr - br * pi
        if extra is not None:
            grad_r = grad_r + part(extra, 0, rows, w)
            grad_i = grad_i + part(extra, 1, rows, w)
        put(out, 0, rows, grad_r)
        put(out, 1, rows, grad_i)


def gathered(head, place, tile, one, both, kept):
    w = kept.shape[2]

    def window(row, rows):
        first_way, second_way = ways_of(head, rows, w, row)
        a, b = first_way(place), second_way(place)
        values = []
        for plane in range(2):
            near = jnp.where(a, part(one, plane, rows, w), part(tile, plane, rows, w))
            value = jnp.where(b, part(both, plane, rows, w), near)
            kept[plane, rows, :] = value
            values.append(value)
        return values

    return window


def updated(head, place, edge_row, edge_col, kept, own, minus, plus):
    odd = odd_row(place)
    w = kept.shape[2]

    def window(row, rows):
        i, j = indices(rows, w, row)
        a, b = low(i, place), far(j, place)
        outside = (a & absent(edge_row)) | (b & absent(edge_col))
        second = b if head else a
        values = []
        for plane in range(2):
            low_side, high_side = part(minus, plane, rows, w), part(plus, plane, rows, w)
            if not head:
                low_side, high_side = pick(odd, low_side, high_side), pick(odd, high_side, low_side)
            near = jnp.where(second, high_side, low_side)
            value = kept[plane, rows, :] - STEP * (own[plane, rows, :] + near)
            values.append(jnp.where(outside, 0.0, value))
        return values

    return window


def open_first(first, place, tile, one, both, pupil, bx, byt, kept, acc, right_of, left, half):
    right_product(first, gathered(True, place, tile, one, both, kept), pupil, bx, left, half)
    acc[...] = dot(byt[...], half[...])
    right_of[...] = both[-1][:, both[-1].shape[1] - EXTRA :, :]


def close_first(
    first, live, place, tile, one, both, acc, pupil, amp, bx, byt, bxt, by, kept, under, stacked, out, left, half
):
    right_product(first, gathered(False, place, tile, one, both, kept), pupil, bx, left, half)
    finish(acc, byt, half, amp, live, bxt, left, stacked)
    back(0, by, stacked, pupil, out, None)
    under[...] = both[:, both.shape[1] - EXTRA :, :]


def open_second(
    first, place, edge_row, edge_col, kept, own, minus, plus, pupil, bx, byt, acc, left, half
):
    window = updated(True, place, edge_row, edge_col, kept, own, minus, plus)
    right_product(first, window, pupil, bx, left, half)
    acc[...] = dot(byt[...], half[...])


def close_second(
    first, live, place, edge_row, edge_col, kept, own, minus, plus, acc, pupil, amp, bx, byt, bxt, by,
    extra, stacked, out, left, half
):
    window = updated(False, place, edge_row, edge_col, kept, own, minus, plus)
    right_product(first, window, pupil, bx, left, half)
    finish(acc, byt, half, amp, live, bxt, left, stacked)
    back(0, by, stacked, pupil, out, extra)


def rest_first(first, by, stacked, pupil, out):
    back(first, by, stacked, pupil, out, None)


def rest_second(first, by, stacked, pupil, extra, out):
    back(first, by, stacked, pupil, out, extra)


def compose_kernel(first, head, me, target, tile, one, out):
    w = me.shape[2]
    for row, rows in split(first, w):
        mask = ways_of(head, rows, w, row)[0](target)
        for plane in range(2):
            value = jnp.where(mask, part(one, plane, rows, w), part(tile, plane, rows, w))
            put(out, plane, rows, value)
    end = out[-1] if head else out
    end[:, end.shape[1] - EXTRA :, :] = me[...]


def pick(odd, when_odd, when_even):
    return jnp.where(odd, when_odd, when_even)


def between_kernel(
    first, head, me, minus, plus, target_minus, target_plus, mine, got_minus, got_plus, to_minus, to_plus
):
    w = me.shape[2]
    odd = odd_row(me)
    for row, rows in split(first, w):
        ways = ways_of(head, rows, w, row)
        f, f_minus, f_plus = (ways[0](x) for x in (me, minus, plus))
        s, s_minus, s_plus = (ways[1](x) for x in (me, minus, plus))

        def seen(goal):
            return f == goal, ~goal & f_minus, goal & ~f_plus

        minus_m = [a & ~b for a, b in zip(seen(ways[0](target_minus)), (s, s_minus, s_plus))]
        plus_m = [a & b for a, b in zip(seen(ways[0](target_plus)), (s, s_minus, s_plus))]
        for plane in range(2):
            values = [part(x, plane, rows, w) for x in (mine, got_minus, got_plus)]
            if head:
                values[1:] = pick(odd, values[1], values[2]), pick(odd, values[2], values[1])
            sums = []
            for masks in (minus_m, plus_m):
                terms = [jnp.where(m, v, 0.0) for m, v in zip(masks, values)]
                sums.append(terms[0] + terms[1] + terms[2])
            if not head:
                sums = pick(odd, sums[0], sums[1]), pick(odd, sums[1], sums[0])
            put(to_minus, plane, rows, sums[0])
            put(to_plus, plane, rows, sums[1])


def own_kernel(first, head, me, minus, plus, mine, got_minus, got_plus, own):
    w = me.shape[2]
    odd = odd_row(me)
    for row, rows in split(first, w):
        ways = ways_of(head, rows, w, row)
        f, f_minus, f_plus = (ways[0](x) for x in (me, minus, plus))
        s, s_minus, s_plus = (ways[1](x) for x in (me, minus, plus))
        own_minus, own_plus = ~f & f_minus & (s == s_minus), f & ~f_plus & (s == s_plus)
        for plane in range(2):
            values = [part(x, plane, rows, w) for x in (mine, got_minus, got_plus)]
            if head:
                values[1:] = pick(odd, values[1], values[2]), pick(odd, values[2], values[1])
            others = jnp.where(own_minus, values[1], 0.0) + jnp.where(own_plus, values[2], 0.0)
            put(own, plane, rows, values[0] + others)


def final_kernel(first, head, me, minus, tile, mine, got, to_plus, base):
    w = me.shape[2]
    for row, rows in split(first, w):
        ways = ways_of(head, rows, w, row)
        f, f_minus = ways[0](me), ways[0](minus)
        s, s_minus = ways[1](me), ways[1](minus)
        for plane in range(2):
            own = jnp.where(f, 0.0, part(mine, plane, rows, w))
            other = jnp.where(f_minus, part(got, plane, rows, w), 0.0)
            put(to_plus, plane, rows, jnp.where(s, own, 0.0) + jnp.where(s_minus, other, 0.0))
            kept = jnp.where(s, 0.0, own) + jnp.where(s_minus, 0.0, other)
            base[plane, rows, :] = part(tile, plane, rows, w) - STEP * kept


def store(first, base, got, whole, previous=None):
    _, h, w = base.shape
    held = () if previous is None else (previous,)
    got = got if isinstance(got, list) else [got]

    def kernel(base, *refs):
        pieces = refs[: len(got)]
        out, value, sems = refs[-3:]
        copies, row = [], 0
        for k, piece in enumerate(pieces):
            size = min(piece.shape[1], h - row)
            rows = slice(row, row + size)
            value[:, rows, :] = base[:, rows, :] - STEP * piece[:, :size, :]
            copy = pltpu.make_async_copy(
                value.at[:, pl.ds(row, size), :], out.at[:, pl.ds(first + row, size), :], sems.at[k]
            )
            copy.start()
            copies.append(copy)
            row += size
        for copy in copies:
            copy.wait()

    return pl.pallas_call(
        kernel,
        out_shape=whole,
        in_specs=[VMEM] * (1 + len(got)) + [ANY] * len(held),
        out_specs=ANY,
        scratch_shapes=[pltpu.VMEM((2, h, w), F32), pltpu.SemaphoreType.DMA((len(got),))],
        input_output_aliases={1 + len(got): 0} if held else {},
        compiler_params=pltpu.CompilerParams(vmem_limit_bytes=LIMIT),
    )(base, *got, *held)


def on_device(spectrum, pupil, amplitudes, offsets, counts):
    w = pupil.shape[1]
    h = w // 2
    amp = amplitudes[0, 0, 0]
    offset = offsets[0, 0]

    def block(rows):
        return jax.ShapeDtypeStruct((2, rows, w), F32)

    half, whole, spot = block(h), block(w), block(EXTRA)
    pieces = [block(h // 2)] * 2
    odd = lax.axis_index("row") % 2 * ODD
    spots = offset[0] + 1 + jnp.stack([odd, jnp.zeros_like(odd)])
    me = jnp.broadcast_to(spots.astype(F32)[:, None, None], (2, EXTRA, w))
    head = spectrum[:, :h]
    tail = [spectrum[:, h : h + h // 2], spectrum[:, h + h // 2 :]]

    def each(values, axis, steps):
        return [shifted(value, axis, steps) for value in values]

    head_below = shifted(head, "row", -1)
    tail_right = each(tail, "col", -1)
    above = shifted(me, "row", 1)
    left_of = shifted(me, "col", 1)

    cosine, sine = dft_tables(w)
    square = jax.ShapeDtypeStruct((2 * w, 2 * w), BF16)
    stack = jax.ShapeDtypeStruct((2 * w, w), BF16)
    bx, bxt, by, byt_head, byt_tail, rolled = call(
        prepare_kernel, [square] * 3 + [stack] * 2 + [whole], (cosine, sine, pupil), scalars=(offset,)
    )

    (tail_made,) = call(
        functools.partial(compose_kernel, h, False), [block(h + EXTRA)], (me, above, tail, tail_right)
    )
    tail_both = shifted(tail_made, "row", -1)
    (head_made,) = call(
        functools.partial(compose_kernel, 0, True),
        [[pieces[0], block(h // 2 + EXTRA)]],
        (me, left_of, head, head_below),
        after=(tail_made,),
    )
    head_both = each(head_made, "col", -1)

    total = jax.ShapeDtypeStruct((2 * w, w), F32)
    products = pltpu.VMEM((w, w), BF16)
    left_half, left_whole = pltpu.VMEM((h, 2 * w), BF16), pltpu.VMEM((w, 2 * w), BF16)
    head_kept, acc, right_of = call(
        functools.partial(open_first, 0),
        [half, total, spot],
        (me, head, head_below, head_both, rolled, bx, byt_head),
        (left_half, products),
    )
    tail_kept, under, stacked, head_grad = call(
        functools.partial(close_first, h),
        [half, spot, stack, block(h + PAD)],
        (me, tail, tail_right, tail_both, acc, rolled, amp, bx, byt_tail, bxt, by),
        (left_whole, products),
        scalars=(counts,),
    )

    got_pairs = [swapped(head_grad, "row", False), swapped(head_grad, "row", True)]
    (tail_grad,) = call(functools.partial(rest_first, h), [[half]], (by, stacked, rolled))
    got_left, got_right = each(tail_grad, "col", 1), each(tail_grad, "col", -1)
    to_even, to_odd = call(
        functools.partial(between_kernel, h, False),
        [block(h + PAD), block(h + PAD)],
        (me, left_of, right_of, above, under, tail_grad, got_left, got_right),
    )
    (tail_own,) = call(
        functools.partial(own_kernel, h, False),
        [half],
        (me, left_of, right_of, tail_grad, got_left, got_right),
        after=(to_even,),
    )
    tail_sums = (tail_own, swapped(to_even, "row", False), swapped(to_odd, "row", True))
    to_left, to_right = call(
        functools.partial(between_kernel, 0, True),
        [[half], [half]],
        (me, above, under, left_of, right_of, head_grad, *got_pairs),
        after=(to_even,),
    )
    (head_own,) = call(
        functools.partial(own_kernel, 0, True),
        [half],
        (me, above, under, head_grad, *got_pairs),
        after=(to_left[0],),
    )
    head_sums = (head_own, each(to_right, "col", 1), each(to_left, "col", -1))

    (acc,) = call(
        functools.partial(open_second, 0),
        [total],
        (me, under, right_of, head_kept, *head_sums, rolled, bx, byt_head),
        (left_half, products),
    )
    stacked, head_total = call(
        functools.partial(close_second, h),
        [stack, half],
        (me, under, right_of, tail_kept, *tail_sums, acc, rolled, amp, bx, byt_tail, bxt, by, head_grad),
        (left_whole, products),
        scalars=(counts,),
    )

    head_above = shifted(head_total, "row", 1)
    (tail_total,) = call(
        functools.partial(rest_second, h), [pieces], (by, stacked, rolled, tail_grad)
    )
    tail_left = each(tail_total, "col", 1)
    tail_down, tail_base = call(
        functools.partial(final_kernel, h, False), [half, half], (me, left_of, tail, tail_total, tail_left)
    )
    tail_got = shifted(tail_down, "row", 1)
    head_right, head_base = call(
        functools.partial(final_kernel, 0, True),
        [pieces, half],
        (me, above, head, head_total, head_above),
        after=(tail_down,),
    )
    head_got = each(head_right, "col", 1)
    partial = store(0, head_base, head_got, whole)
    return store(h, tail_base, tail_got, whole, partial)


def solution(mesh):
    in_specs = (
        P(None, "row", "col"),
        P(),
        P("row", "col", None, None, None),
        P("row", "col", None, None),
        P("row", "col"),
    )
    out_specs = P(None, "row", "col")
    return jax.shard_map(
        on_device, mesh=mesh, in_specs=in_specs, out_specs=out_specs, check_vma=False
    )
```

```python
import functools
import math

import jax
import jax.numpy as jnp
from jax import lax
from jax.experimental import pallas as pl
from jax.experimental.pallas import tpu as pltpu
from jax.sharding import PartitionSpec as P

STEP = 0.5
FLOOR = 0.05
VMEM = pl.BlockSpec(memory_space=pltpu.VMEM)
ANY = pl.BlockSpec(memory_space=pl.ANY)
SMEM = pl.BlockSpec(memory_space=pltpu.SMEM)
LIMIT = 12 * 1024 * 1024
F32 = jnp.float32
BF16 = jnp.bfloat16

EXTRA = 8
BLOCK = 128
ODD = 1024
PAD = 8


def shifted(value, axis, steps):
    count = lax.axis_size(axis)
    leading, last = (max(0, -steps), min(count, count - steps))
    return lax.ppermute(value, axis, [(source, source + steps) for source in range(leading, last)])


def swapped(value, axis, odd):
    lower = range(1 if odd else 0, lax.axis_size(axis) - 1, 2)
    return lax.ppermute(value, axis, [(a, a + 1) for a in lower] + [(a + 1, a) for a in lower])


def dft_tables(width):
    index = jnp.arange(width, dtype=jnp.int32)
    phase = index[:, None] * index[None, :] % width
    angle = phase.astype(jnp.float32) * (2.0 * math.pi / width)
    scale = 1.0 / math.sqrt(width)
    return (
        (jnp.cos(angle) * scale).astype(jnp.bfloat16),
        (jnp.sin(angle) * scale).astype(jnp.bfloat16),
    )


def call(kernel, outs, arrays, scratch=(), scalars=(), after=()):
    flat, tree = jax.tree.flatten(tuple(arrays))
    out_flat, out_tree = jax.tree.flatten(tuple(outs))
    skip, count = len(after), len(scalars)

    def body(*refs):
        refs = refs[skip:]
        numbers, refs = refs[:count], refs[count:]
        given = jax.tree.unflatten(tree, refs[: len(flat)])
        made = jax.tree.unflatten(out_tree, refs[len(flat) : len(flat) + len(out_flat)])
        kernel(*numbers, *given, *made, *refs[len(flat) + len(out_flat) :])

    results = pl.pallas_call(
        body,
        out_shape=out_flat,
        in_specs=[ANY] * skip + [SMEM] * count + [VMEM] * len(flat),
        out_specs=[VMEM] * len(out_flat),
        scratch_shapes=list(scratch),
        compiler_params=pltpu.CompilerParams(vmem_limit_bytes=LIMIT),
    )(*after, *scalars, *flat)
    return jax.tree.unflatten(out_tree, results)


def split(first, width):
    return [(first + row, slice(row, row + BLOCK)) for row in range(0, width // 2, BLOCK)]


def place_in(half, rows, width):
    if not isinstance(half, list):
        return half, rows
    height = width // 2 // len(half)
    index = rows.start // height
    return half[index], slice(rows.start - index * height, rows.stop - index * height)


def part(half, plane, rows, width):
    array, inner = place_in(half, rows, width)
    return array[plane, inner, :]


def put(half, plane, rows, value):
    array, inner = place_in(half, rows, value.shape[1])
    array[plane, inner, :] = value


def indices(rows, width, first):
    shape = (rows.stop - rows.start, width)
    return (
        lax.broadcasted_iota(jnp.int32, shape, 0) + first,
        lax.broadcasted_iota(jnp.int32, shape, 1),
    )


def low(i, place):
    return i + 1 < (place[0, :1, :].astype(jnp.int32) & (ODD - 1))


def far(j, place):
    return j + 1 < place[1, :1, :].astype(jnp.int32)


def ways_of(head, rows, width, first):
    i, j = indices(rows, width, first)
    pair = (functools.partial(low, i), functools.partial(far, j))
    return pair if head else pair[::-1]


def odd_row(place):
    return place[0, :1, :] >= ODD


def absent(place):
    return place[0, :1, :] == 0.0


def place_kernel(offset, out):
    odd = lax.rem(lax.axis_index("row"), 2) * ODD
    for plane, add in ((0, odd), (1, 0)):
        out[plane] = jnp.full(out.shape[1:], offset[0, plane] + 1 + add, jnp.int32).astype(F32)


def prepare_kernel(offset, cos_ref, sin_ref, pupil_ref, bx, bxt, by, byt_head, byt_tail, pupil_out):
    w = cos_ref.shape[0]
    h = w // 2
    cosine = cos_ref[...].astype(F32)
    sine = sin_ref[...].astype(F32)
    oy, ox = offset[0, 0], offset[0, 1]

    def rolled(value, shift, axis):
        return pltpu.roll(value, shift, axis)

    c, s = rolled(cosine, ox, 0).astype(BF16), rolled(sine, ox, 0).astype(BF16)
    bx[:w, :w], bx[:w, w:], bx[w:, :w], bx[w:, w:] = c, s, -s, c
    c, s = rolled(cosine, ox, 1).astype(BF16), rolled(sine, ox, 1).astype(BF16)
    bxt[:w, :w], bxt[:w, w:], bxt[w:, :w], bxt[w:, w:] = c, -s, s, c
    c, s = rolled(cosine, oy, 0).astype(BF16), rolled(sine, oy, 0).astype(BF16)
    by[:w, :w], by[:w, w:], by[w:, :w], by[w:, w:] = c, s, -s, c
    c, s = rolled(cosine, oy, 1).astype(BF16), rolled(sine, oy, 1).astype(BF16)
    for out, cols in ((byt_head, slice(0, h)), (byt_tail, slice(h, w))):
        n = cols.stop - cols.start
        out[:w, :n], out[:w, n:] = c[:, cols], -s[:, cols]
        out[w:, :n], out[w:, n:] = s[:, cols], c[:, cols]
    for plane in range(2):
        pupil_out[plane] = rolled(rolled(pupil_ref[plane], oy, 0), ox, 1)


def dot(a, b):
    return jnp.dot(a, b, preferred_element_type=F32)


def right_product(first, window, pupil, bx, left, half):
    w = bx.shape[0] // 2
    h = half.shape[0] // 2
    for row, rows in split(first, w):
        wr, wi = window(row, rows)
        across = slice(row, row + rows.stop - rows.start)
        pr, pi = pupil[0, across, :], pupil[1, across, :]
        left[rows, :w] = (wr * pr - wi * pi).astype(BF16)
        left[rows, w:] = (wr * pi + wi * pr).astype(BF16)
    half[:h, :] = dot(left[:h, :], bx[:, :w]).astype(BF16)
    half[h:, :] = dot(left[:h, :], bx[:, w:]).astype(BF16)


def finish(acc, byt_tail, half, amp, live, bxt, left, stacked):
    w = amp.shape[0]
    block = 256
    alive = (live[0, 0] > 0).astype(F32)
    for first in range(0, w, block):
        rows = slice(first, first + block)
        lower = slice(w + first, w + first + block)
        wave_r = acc[rows, :] + dot(byt_tail[rows, :], half[...])
        wave_i = acc[lower, :] + dot(byt_tail[lower, :], half[...])
        power = jnp.maximum(wave_r * wave_r + wave_i * wave_i, FLOOR * FLOOR)
        keep = (1.0 - amp[rows, :] * lax.rsqrt(power)) * alive
        left[rows, :w] = (wave_r * keep).astype(BF16)
        left[rows, w:] = (wave_i * keep).astype(BF16)
    stacked[:w, :] = dot(left[...], bxt[:, :w]).astype(BF16)
    stacked[w:, :] = dot(left[...], bxt[:, w:]).astype(BF16)


def back(first, by, stacked, pupil, out, extra):
    w = stacked.shape[1]
    h = w // 2
    back_r = dot(by[first : first + h, :], stacked[...])
    back_i = dot(by[w + first : w + first + h, :], stacked[...])
    for row, rows in split(first, w):
        across = slice(row, row + rows.stop - rows.start)
        pr, pi = pupil[0, across, :], pupil[1, across, :]
        br, bi = back_r[rows, :], back_i[rows, :]
        grad_r = br * pr + bi * pi
        grad_i = bi * pr - br * pi
        if extra is not None:
            grad_r = grad_r + part(extra, 0, rows, w)
            grad_i = grad_i + part(extra, 1, rows, w)
        put(out, 0, rows, grad_r)
        put(out, 1, rows, grad_i)


def gathered(head, place, tile, one, both, kept):
    w = kept.shape[2]

    def window(row, rows):
        first_way, second_way = ways_of(head, rows, w, row)
        a, b = first_way(place), second_way(place)
        values = []
        for plane in range(2):
            near = jnp.where(a, part(one, plane, rows, w), part(tile, plane, rows, w))
            value = jnp.where(b, part(both, plane, rows, w), near)
            kept[plane, rows, :] = value
            values.append(value)
        return values

    return window


def updated(head, place, edge_row, edge_col, kept, own, minus, plus):
    odd = odd_row(place)
    w = kept.shape[2]

    def window(row, rows):
        i, j = indices(rows, w, row)
        a, b = low(i, place), far(j, place)
        outside = (a & absent(edge_row)) | (b & absent(edge_col))
        second = b if head else a
        values = []
        for plane in range(2):
            low_side, high_side = part(minus, plane, rows, w), part(plus, plane, rows, w)
            if not head:
                low_side, high_side = pick(odd, low_side, high_side), pick(odd, high_side, low_side)
            near = jnp.where(second, high_side, low_side)
            value = kept[plane, rows, :] - STEP * (own[plane, rows, :] + near)
            values.append(jnp.where(outside, 0.0, value))
        return values

    return window


def open_first(first, place, tile, one, both, pupil, bx, byt, kept, acc, right_of, left, half):
    right_product(first, gathered(True, place, tile, one, both, kept), pupil, bx, left, half)
    acc[...] = dot(byt[...], half[...])
    right_of[...] = both[-1][:, both[-1].shape[1] - EXTRA :, :]


def close_first(
    first, live, place, tile, one, both, acc, pupil, amp, bx, byt, bxt, by, kept, under, stacked, out, left, half
):
    right_product(first, gathered(False, place, tile, one, both, kept), pupil, bx, left, half)
    finish(acc, byt, half, amp, live, bxt, left, stacked)
    back(0, by, stacked, pupil, out, None)
    under[...] = both[:, both.shape[1] - EXTRA :, :]


def open_second(
    first, place, edge_row, edge_col, kept, own, minus, plus, pupil, bx, byt, acc, left, half
):
    window = updated(True, place, edge_row, edge_col, kept, own, minus, plus)
    right_product(first, window, pupil, bx, left, half)
    acc[...] = dot(byt[...], half[...])


def close_second(
    first, live, place, edge_row, edge_col, kept, own, minus, plus, acc, pupil, amp, bx, byt, bxt, by,
    extra, stacked, out, left, half
):
    window = updated(False, place, edge_row, edge_col, kept, own, minus, plus)
    right_product(first, window, pupil, bx, left, half)
    finish(acc, byt, half, amp, live, bxt, left, stacked)
    back(0, by, stacked, pupil, out, extra)


def rest_first(first, by, stacked, pupil, out):
    back(first, by, stacked, pupil, out, None)


def rest_second(first, by, stacked, pupil, extra, out):
    back(first, by, stacked, pupil, out, extra)


def compose_kernel(first, head, me, target, tile, one, out):
    w = me.shape[2]
    for row, rows in split(first, w):
        mask = ways_of(head, rows, w, row)[0](target)
        for plane in range(2):
            value = jnp.where(mask, part(one, plane, rows, w), part(tile, plane, rows, w))
            put(out, plane, rows, value)
    end = out[-1] if head else out
    end[:, end.shape[1] - EXTRA :, :] = me[...]


def pick(odd, when_odd, when_even):
    return jnp.where(odd, when_odd, when_even)


def between_kernel(
    first, head, me, minus, plus, target_minus, target_plus, mine, got_minus, got_plus, to_minus, to_plus
):
    w = me.shape[2]
    odd = odd_row(me)
    for row, rows in split(first, w):
        ways = ways_of(head, rows, w, row)
        f, f_minus, f_plus = (ways[0](x) for x in (me, minus, plus))
        s, s_minus, s_plus = (ways[1](x) for x in (me, minus, plus))

        def seen(goal):
            return f == goal, ~goal & f_minus, goal & ~f_plus

        minus_m = [a & ~b for a, b in zip(seen(ways[0](target_minus)), (s, s_minus, s_plus))]
        plus_m = [a & b for a, b in zip(seen(ways[0](target_plus)), (s, s_minus, s_plus))]
        for plane in range(2):
            values = [part(x, plane, rows, w) for x in (mine, got_minus, got_plus)]
            if head:
                values[1:] = pick(odd, values[1], values[2]), pick(odd, values[2], values[1])
            sums = []
            for masks in (minus_m, plus_m):
                terms = [jnp.where(m, v, 0.0) for m, v in zip(masks, values)]
                sums.append(terms[0] + terms[1] + terms[2])
            if not head:
                sums = pick(odd, sums[0], sums[1]), pick(odd, sums[1], sums[0])
            put(to_minus, plane, rows, sums[0])
            put(to_plus, plane, rows, sums[1])


def own_kernel(first, head, me, minus, plus, mine, got_minus, got_plus, own):
    w = me.shape[2]
    odd = odd_row(me)
    for row, rows in split(first, w):
        ways = ways_of(head, rows, w, row)
        f, f_minus, f_plus = (ways[0](x) for x in (me, minus, plus))
        s, s_minus, s_plus = (ways[1](x) for x in (me, minus, plus))
        own_minus, own_plus = ~f & f_minus & (s == s_minus), f & ~f_plus & (s == s_plus)
        for plane in range(2):
            values = [part(x, plane, rows, w) for x in (mine, got_minus, got_plus)]
            if head:
                values[1:] = pick(odd, values[1], values[2]), pick(odd, values[2], values[1])
            others = jnp.where(own_minus, values[1], 0.0) + jnp.where(own_plus, values[2], 0.0)
            put(own, plane, rows, values[0] + others)


def final_kernel(first, head, me, minus, tile, mine, got, to_plus, base):
    w = me.shape[2]
    for row, rows in split(first, w):
        ways = ways_of(head, rows, w, row)
        f, f_minus = ways[0](me), ways[0](minus)
        s, s_minus = ways[1](me), ways[1](minus)
        for plane in range(2):
            own = jnp.where(f, 0.0, part(mine, plane, rows, w))
            other = jnp.where(f_minus, part(got, plane, rows, w), 0.0)
            put(to_plus, plane, rows, jnp.where(s, own, 0.0) + jnp.where(s_minus, other, 0.0))
            kept = jnp.where(s, 0.0, own) + jnp.where(s_minus, 0.0, other)
            base[plane, rows, :] = part(tile, plane, rows, w) - STEP * kept


def store(first, base, got, whole, previous=None):
    _, h, w = base.shape
    held = () if previous is None else (previous,)
    got = got if isinstance(got, list) else [got]

    def kernel(base, *refs):
        pieces = refs[: len(got)]
        out, value, sems = refs[-3:]
        copies, row = [], 0
        for k, piece in enumerate(pieces):
            size = min(piece.shape[1], h - row)
            rows = slice(row, row + size)
            value[:, rows, :] = base[:, rows, :] - STEP * piece[:, :size, :]
            copy = pltpu.make_async_copy(
                value.at[:, pl.ds(row, size), :], out.at[:, pl.ds(first + row, size), :], sems.at[k]
            )
            copy.start()
            copies.append(copy)
            row += size
        for copy in copies:
            copy.wait()

    return pl.pallas_call(
        kernel,
        out_shape=whole,
        in_specs=[VMEM] * (1 + len(got)) + [ANY] * len(held),
        out_specs=ANY,
        scratch_shapes=[pltpu.VMEM((2, h, w), F32), pltpu.SemaphoreType.DMA((len(got),))],
        input_output_aliases={1 + len(got): 0} if held else {},
        compiler_params=pltpu.CompilerParams(vmem_limit_bytes=LIMIT),
    )(base, *got, *held)


def on_device(spectrum, pupil, amplitudes, offsets, counts):
    w = pupil.shape[1]
    h = w // 2
    amp = amplitudes[0, 0, 0]
    offset = offsets[0, 0]

    def block(rows):
        return jax.ShapeDtypeStruct((2, rows, w), F32)

    half, whole, spot = block(h), block(w), block(EXTRA)
    pieces = [block(h // 2)] * 2
    (me,) = call(place_kernel, [spot], (), scalars=(offset,))
    head = spectrum[:, :h]
    tail = [spectrum[:, h : h + h // 2], spectrum[:, h + h // 2 :]]

    def each(values, axis, steps):
        return [shifted(value, axis, steps) for value in values]

    head_below = shifted(head, "row", -1)
    tail_right = each(tail, "col", -1)
    above = shifted(me, "row", 1)
    left_of = shifted(me, "col", 1)

    cosine, sine = dft_tables(w)
    square = jax.ShapeDtypeStruct((2 * w, 2 * w), BF16)
    stack = jax.ShapeDtypeStruct((2 * w, w), BF16)
    bx, bxt, by, byt_head, byt_tail, rolled = call(
        prepare_kernel, [square] * 3 + [stack] * 2 + [whole], (cosine, sine, pupil), scalars=(offset,)
    )

    (tail_made,) = call(
        functools.partial(compose_kernel, h, False), [block(h + EXTRA)], (me, above, tail, tail_right)
    )
    tail_both = shifted(tail_made, "row", -1)
    (head_made,) = call(
        functools.partial(compose_kernel, 0, True),
        [[pieces[0], block(h // 2 + EXTRA)]],
        (me, left_of, head, head_below),
        after=(tail_made,),
    )
    head_both = each(head_made, "col", -1)

    total = jax.ShapeDtypeStruct((2 * w, w), F32)
    products = pltpu.VMEM((w, w), BF16)
    left_half, left_whole = pltpu.VMEM((h, 2 * w), BF16), pltpu.VMEM((w, 2 * w), BF16)
    head_kept, acc, right_of = call(
        functools.partial(open_first, 0),
        [half, total, spot],
        (me, head, head_below, head_both, rolled, bx, byt_head),
        (left_half, products),
    )
    tail_kept, under, stacked, head_grad = call(
        functools.partial(close_first, h),
        [half, spot, stack, block(h + PAD)],
        (me, tail, tail_right, tail_both, acc, rolled, amp, bx, byt_tail, bxt, by),
        (left_whole, products),
        scalars=(counts,),
    )

    got_pairs = [swapped(head_grad, "row", False), swapped(head_grad, "row", True)]
    (tail_grad,) = call(functools.partial(rest_first, h), [[half]], (by, stacked, rolled))
    got_left, got_right = each(tail_grad, "col", 1), each(tail_grad, "col", -1)
    to_even, to_odd = call(
        functools.partial(between_kernel, h, False),
        [block(h + PAD), block(h + PAD)],
        (me, left_of, right_of, above, under, tail_grad, got_left, got_right),
    )
    (tail_own,) = call(
        functools.partial(own_kernel, h, False),
        [half],
        (me, left_of, right_of, tail_grad, got_left, got_right),
        after=(to_even,),
    )
    tail_sums = (tail_own, swapped(to_even, "row", False), swapped(to_odd, "row", True))
    to_left, to_right = call(
        functools.partial(between_kernel, 0, True),
        [[half], [half]],
        (me, above, under, left_of, right_of, head_grad, *got_pairs),
        after=(to_even,),
    )
    (head_own,) = call(
        functools.partial(own_kernel, 0, True),
        [half],
        (me, above, under, head_grad, *got_pairs),
        after=(to_left[0],),
    )
    head_sums = (head_own, each(to_right, "col", 1), each(to_left, "col", -1))

    (acc,) = call(
        functools.partial(open_second, 0),
        [total],
        (me, under, right_of, head_kept, *head_sums, rolled, bx, byt_head),
        (left_half, products),
    )
    stacked, head_total = call(
        functools.partial(close_second, h),
        [stack, half],
        (me, under, right_of, tail_kept, *tail_sums, acc, rolled, amp, bx, byt_tail, bxt, by, head_grad),
        (left_whole, products),
        scalars=(counts,),
    )

    head_above = shifted(head_total, "row", 1)
    (tail_total,) = call(
        functools.partial(rest_second, h), [pieces], (by, stacked, rolled, tail_grad)
    )
    tail_left = each(tail_total, "col", 1)
    tail_down, tail_base = call(
        functools.partial(final_kernel, h, False), [half, half], (me, left_of, tail, tail_total, tail_left)
    )
    tail_got = shifted(tail_down, "row", 1)
    head_right, head_base = call(
        functools.partial(final_kernel, 0, True),
        [pieces, half],
        (me, above, head, head_total, head_above),
        after=(tail_down,),
    )
    head_got = each(head_right, "col", 1)
    partial = store(0, head_base, head_got, whole)
    return store(h, tail_base, tail_got, whole, partial)


def solution(mesh):
    in_specs = (
        P(None, "row", "col"),
        P(),
        P("row", "col", None, None, None),
        P("row", "col", None, None),
        P("row", "col"),
    )
    out_specs = P(None, "row", "col")
    return jax.shard_map(
        on_device, mesh=mesh, in_specs=in_specs, out_specs=out_specs, check_vma=False
    )
```

```python
import functools
import math

import jax
import jax.numpy as jnp
from jax import lax
from jax.experimental import pallas as pl
from jax.experimental.pallas import tpu as pltpu
from jax.sharding import PartitionSpec as P

STEP = 0.5
FLOOR = 0.05
VMEM = pl.BlockSpec(memory_space=pltpu.VMEM)
ANY = pl.BlockSpec(memory_space=pl.ANY)
SMEM = pl.BlockSpec(memory_space=pltpu.SMEM)
LIMIT = 12 * 1024 * 1024
F32 = jnp.float32
BF16 = jnp.bfloat16

EXTRA = 8
BLOCK = 128
STORES = 4
ODD = 1024
PAD = 8


def shifted(value, axis, steps):
    count = lax.axis_size(axis)
    leading, last = (max(0, -steps), min(count, count - steps))
    return lax.ppermute(value, axis, [(source, source + steps) for source in range(leading, last)])


def swapped(value, axis, odd):
    lower = range(1 if odd else 0, lax.axis_size(axis) - 1, 2)
    return lax.ppermute(value, axis, [(a, a + 1) for a in lower] + [(a + 1, a) for a in lower])


def dft_tables(width):
    index = jnp.arange(width, dtype=jnp.int32)
    phase = index[:, None] * index[None, :] % width
    angle = phase.astype(jnp.float32) * (2.0 * math.pi / width)
    scale = 1.0 / math.sqrt(width)
    return (
        (jnp.cos(angle) * scale).astype(jnp.bfloat16),
        (jnp.sin(angle) * scale).astype(jnp.bfloat16),
    )


def call(kernel, outs, arrays, scratch=(), scalars=(), after=()):
    flat, tree = jax.tree.flatten(tuple(arrays))
    out_flat, out_tree = jax.tree.flatten(tuple(outs))
    skip, count = len(after), len(scalars)

    def body(*refs):
        refs = refs[skip:]
        numbers, refs = refs[:count], refs[count:]
        given = jax.tree.unflatten(tree, refs[: len(flat)])
        made = jax.tree.unflatten(out_tree, refs[len(flat) : len(flat) + len(out_flat)])
        kernel(*numbers, *given, *made, *refs[len(flat) + len(out_flat) :])

    results = pl.pallas_call(
        body,
        out_shape=out_flat,
        in_specs=[ANY] * skip + [SMEM] * count + [VMEM] * len(flat),
        out_specs=[VMEM] * len(out_flat),
        scratch_shapes=list(scratch),
        compiler_params=pltpu.CompilerParams(vmem_limit_bytes=LIMIT),
    )(*after, *scalars, *flat)
    return jax.tree.unflatten(out_tree, results)


def split(first, width):
    return [(first + row, slice(row, row + BLOCK)) for row in range(0, width // 2, BLOCK)]


def place_in(half, rows, width):
    if not isinstance(half, list):
        return half, rows
    height = width // 2 // len(half)
    index = rows.start // height
    return half[index], slice(rows.start - index * height, rows.stop - index * height)


def part(half, plane, rows, width):
    array, inner = place_in(half, rows, width)
    return array[plane, inner, :]


def put(half, plane, rows, value):
    array, inner = place_in(half, rows, value.shape[1])
    array[plane, inner, :] = value


def indices(rows, width, first):
    shape = (rows.stop - rows.start, width)
    return (
        lax.broadcasted_iota(jnp.int32, shape, 0) + first,
        lax.broadcasted_iota(jnp.int32, shape, 1),
    )


def low(i, place):
    return i + 1 < (place[0, :1, :].astype(jnp.int32) & (ODD - 1))


def far(j, place):
    return j + 1 < place[1, :1, :].astype(jnp.int32)


def ways_of(head, rows, width, first):
    i, j = indices(rows, width, first)
    pair = (functools.partial(low, i), functools.partial(far, j))
    return pair if head else pair[::-1]


def odd_row(place):
    return place[0, :1, :] >= ODD


def absent(place):
    return place[0, :1, :] == 0.0


def place_kernel(offset, out):
    odd = lax.rem(lax.axis_index("row"), 2) * ODD
    for plane, add in ((0, odd), (1, 0)):
        out[plane] = jnp.full(out.shape[1:], offset[0, plane] + 1 + add, jnp.int32).astype(F32)


def prepare_kernel(offset, cos_ref, sin_ref, pupil_ref, bx, bxt, by, byt_head, byt_tail, pupil_out):
    w = cos_ref.shape[0]
    h = w // 2
    cosine = cos_ref[...].astype(F32)
    sine = sin_ref[...].astype(F32)
    oy, ox = offset[0, 0], offset[0, 1]

    def rolled(value, shift, axis):
        return pltpu.roll(value, shift, axis)

    c, s = rolled(cosine, ox, 0).astype(BF16), rolled(sine, ox, 0).astype(BF16)
    bx[:w, :w], bx[:w, w:], bx[w:, :w], bx[w:, w:] = c, s, -s, c
    c, s = rolled(cosine, ox, 1).astype(BF16), rolled(sine, ox, 1).astype(BF16)
    bxt[:w, :w], bxt[:w, w:], bxt[w:, :w], bxt[w:, w:] = c, -s, s, c
    c, s = rolled(cosine, oy, 0).astype(BF16), rolled(sine, oy, 0).astype(BF16)
    by[:w, :w], by[:w, w:], by[w:, :w], by[w:, w:] = c, s, -s, c
    c, s = rolled(cosine, oy, 1).astype(BF16), rolled(sine, oy, 1).astype(BF16)
    for out, cols in ((byt_head, slice(0, h)), (byt_tail, slice(h, w))):
        n = cols.stop - cols.start
        out[:w, :n], out[:w, n:] = c[:, cols], -s[:, cols]
        out[w:, :n], out[w:, n:] = s[:, cols], c[:, cols]
    for plane in range(2):
        pupil_out[plane] = rolled(rolled(pupil_ref[plane], oy, 0), ox, 1)


def dot(a, b):
    return jnp.dot(a, b, preferred_element_type=F32)


def right_product(first, window, pupil, bx, left, half):
    w = bx.shape[0] // 2
    h = half.shape[0] // 2
    for row, rows in split(first, w):
        wr, wi = window(row, rows)
        across = slice(row, row + rows.stop - rows.start)
        pr, pi = pupil[0, across, :], pupil[1, across, :]
        left[rows, :w] = (wr * pr - wi * pi).astype(BF16)
        left[rows, w:] = (wr * pi + wi * pr).astype(BF16)
    half[:h, :] = dot(left[:h, :], bx[:, :w]).astype(BF16)
    half[h:, :] = dot(left[:h, :], bx[:, w:]).astype(BF16)


def finish(acc, byt_tail, half, amp, live, bxt, left, stacked):
    w = amp.shape[0]
    block = 256
    alive = (live[0, 0] > 0).astype(F32)
    for first in range(0, w, block):
        rows = slice(first, first + block)
        lower = slice(w + first, w + first + block)
        wave_r = acc[rows, :] + dot(byt_tail[rows, :], half[...])
        wave_i = acc[lower, :] + dot(byt_tail[lower, :], half[...])
        power = jnp.maximum(wave_r * wave_r + wave_i * wave_i, FLOOR * FLOOR)
        keep = (1.0 - amp[rows, :] * lax.rsqrt(power)) * alive
        left[rows, :w] = (wave_r * keep).astype(BF16)
        left[rows, w:] = (wave_i * keep).astype(BF16)
    stacked[:w, :] = dot(left[...], bxt[:, :w]).astype(BF16)
    stacked[w:, :] = dot(left[...], bxt[:, w:]).astype(BF16)


def back(first, by, stacked, pupil, out, extra):
    w = stacked.shape[1]
    h = w // 2
    back_r = dot(by[first : first + h, :], stacked[...])
    back_i = dot(by[w + first : w + first + h, :], stacked[...])
    for row, rows in split(first, w):
        across = slice(row, row + rows.stop - rows.start)
        pr, pi = pupil[0, across, :], pupil[1, across, :]
        br, bi = back_r[rows, :], back_i[rows, :]
        grad_r = br * pr + bi * pi
        grad_i = bi * pr - br * pi
        if extra is not None:
            grad_r = grad_r + part(extra, 0, rows, w)
            grad_i = grad_i + part(extra, 1, rows, w)
        put(out, 0, rows, grad_r)
        put(out, 1, rows, grad_i)


def gathered(head, place, tile, one, both, kept):
    w = kept.shape[2]

    def window(row, rows):
        first_way, second_way = ways_of(head, rows, w, row)
        a, b = first_way(place), second_way(place)
        values = []
        for plane in range(2):
            near = jnp.where(a, part(one, plane, rows, w), part(tile, plane, rows, w))
            value = jnp.where(b, part(both, plane, rows, w), near)
            kept[plane, rows, :] = value
            values.append(value)
        return values

    return window


def updated(head, place, edge_row, edge_col, kept, own, minus, plus):
    odd = odd_row(place)
    w = kept.shape[2]

    def window(row, rows):
        i, j = indices(rows, w, row)
        a, b = low(i, place), far(j, place)
        outside = (a & absent(edge_row)) | (b & absent(edge_col))
        second = b if head else a
        values = []
        for plane in range(2):
            low_side, high_side = part(minus, plane, rows, w), part(plus, plane, rows, w)
            if not head:
                low_side, high_side = pick(odd, low_side, high_side), pick(odd, high_side, low_side)
            near = jnp.where(second, high_side, low_side)
            value = kept[plane, rows, :] - STEP * (own[plane, rows, :] + near)
            values.append(jnp.where(outside, 0.0, value))
        return values

    return window


def open_first(first, place, tile, one, both, pupil, bx, byt, kept, acc, right_of, left, half):
    right_product(first, gathered(True, place, tile, one, both, kept), pupil, bx, left, half)
    acc[...] = dot(byt[...], half[...])
    right_of[...] = both[-1][:, both[-1].shape[1] - EXTRA :, :]


def close_first(
    first, live, place, tile, one, both, acc, pupil, amp, bx, byt, bxt, by, kept, under, stacked, out, left, half
):
    right_product(first, gathered(False, place, tile, one, both, kept), pupil, bx, left, half)
    finish(acc, byt, half, amp, live, bxt, left, stacked)
    back(0, by, stacked, pupil, out, None)
    under[...] = both[:, both.shape[1] - EXTRA :, :]


def open_second(
    first, place, edge_row, edge_col, kept, own, minus, plus, pupil, bx, byt, acc, left, half
):
    window = updated(True, place, edge_row, edge_col, kept, own, minus, plus)
    right_product(first, window, pupil, bx, left, half)
    acc[...] = dot(byt[...], half[...])


def close_second(
    first, live, place, edge_row, edge_col, kept, own, minus, plus, acc, pupil, amp, bx, byt, bxt, by,
    extra, stacked, out, left, half
):
    window = updated(False, place, edge_row, edge_col, kept, own, minus, plus)
    right_product(first, window, pupil, bx, left, half)
    finish(acc, byt, half, amp, live, bxt, left, stacked)
    back(0, by, stacked, pupil, out, extra)


def rest_first(first, by, stacked, pupil, out):
    back(first, by, stacked, pupil, out, None)


def rest_second(first, by, stacked, pupil, extra, out):
    back(first, by, stacked, pupil, out, extra)


def compose_kernel(first, head, me, target, tile, one, out):
    w = me.shape[2]
    for row, rows in split(first, w):
        mask = ways_of(head, rows, w, row)[0](target)
        for plane in range(2):
            value = jnp.where(mask, part(one, plane, rows, w), part(tile, plane, rows, w))
            put(out, plane, rows, value)
    end = out[-1] if head else out
    end[:, end.shape[1] - EXTRA :, :] = me[...]


def pick(odd, when_odd, when_even):
    return jnp.where(odd, when_odd, when_even)


def between(
    first, head, me, minus, plus, target_minus, target_plus, mine, got_minus, got_plus, to_minus, to_plus
):
    w = me.shape[2]
    for row, rows in split(first, w):
        ways = ways_of(head, rows, w, row)
        f, f_minus, f_plus = (ways[0](x) for x in (me, minus, plus))
        s, s_minus, s_plus = (ways[1](x) for x in (me, minus, plus))

        def seen(goal):
            return f == goal, ~goal & f_minus, goal & ~f_plus

        minus_m = [a & ~b for a, b in zip(seen(ways[0](target_minus)), (s, s_minus, s_plus))]
        plus_m = [a & b for a, b in zip(seen(ways[0](target_plus)), (s, s_minus, s_plus))]
        for plane in range(2):
            values = [part(x, plane, rows, w) for x in (mine, got_minus, got_plus)]
            sums = []
            for masks in (minus_m, plus_m):
                terms = [jnp.where(m, v, 0.0) for m, v in zip(masks, values)]
                sums.append(terms[0] + terms[1] + terms[2])
            put(to_minus, plane, rows, sums[0])
            put(to_plus, plane, rows, sums[1])


def by_parity(when_odd, when_even):
    odd = lax.rem(lax.axis_index("row"), 2) == 1
    pl.when(odd)(when_odd)
    pl.when(jnp.logical_not(odd))(when_even)


def between_kernel(
    first, head, me, minus, plus, target_minus, target_plus, mine, got_one, got_two, to_one, to_two
):
    places = (me, minus, plus, target_minus, target_plus, mine)
    if head:
        by_parity(
            lambda: between(first, head, *places, got_one, got_two, to_one, to_two),
            lambda: between(first, head, *places, got_two, got_one, to_one, to_two),
        )
    else:
        by_parity(
            lambda: between(first, head, *places, got_one, got_two, to_one, to_two),
            lambda: between(first, head, *places, got_one, got_two, to_two, to_one),
        )


def own_kernel(first, head, me, minus, plus, mine, got_minus, got_plus, own):
    w = me.shape[2]
    odd = odd_row(me)
    for row, rows in split(first, w):
        ways = ways_of(head, rows, w, row)
        f, f_minus, f_plus = (ways[0](x) for x in (me, minus, plus))
        s, s_minus, s_plus = (ways[1](x) for x in (me, minus, plus))
        own_minus, own_plus = ~f & f_minus & (s == s_minus), f & ~f_plus & (s == s_plus)
        for plane in range(2):
            values = [part(x, plane, rows, w) for x in (mine, got_minus, got_plus)]
            if head:
                values[1:] = pick(odd, values[1], values[2]), pick(odd, values[2], values[1])
            others = jnp.where(own_minus, values[1], 0.0) + jnp.where(own_plus, values[2], 0.0)
            put(own, plane, rows, values[0] + others)


def final_kernel(first, head, me, minus, tile, mine, got, to_plus, base):
    w = me.shape[2]
    for row, rows in split(first, w):
        ways = ways_of(head, rows, w, row)
        f, f_minus = ways[0](me), ways[0](minus)
        s, s_minus = ways[1](me), ways[1](minus)
        for plane in range(2):
            own = jnp.where(f, 0.0, part(mine, plane, rows, w))
            other = jnp.where(f_minus, part(got, plane, rows, w), 0.0)
            put(to_plus, plane, rows, jnp.where(s, own, 0.0) + jnp.where(s_minus, other, 0.0))
            kept = jnp.where(s, 0.0, own) + jnp.where(s_minus, 0.0, other)
            base[plane, rows, :] = part(tile, plane, rows, w) - STEP * kept


def store(first, base, got, whole, previous=None):
    _, h, w = base.shape
    held = () if previous is None else (previous,)
    got = got if isinstance(got, list) else [got]

    def kernel(base, *refs):
        pieces = refs[: len(got)]
        out, value, sems = refs[-3:]
        copies = []
        for k in range(STORES):
            size = h // STORES
            rows = slice(k * size, (k + 1) * size)
            for plane in range(2):
                value[plane, rows, :] = base[plane, rows, :] - STEP * part(list(pieces), plane, rows, w)
            copy = pltpu.make_async_copy(
                value.at[:, pl.ds(k * size, size), :], out.at[:, pl.ds(first + k * size, size), :], sems.at[k]
            )
            copy.start()
            copies.append(copy)
        for copy in copies:
            copy.wait()

    return pl.pallas_call(
        kernel,
        out_shape=whole,
        in_specs=[VMEM] * (1 + len(got)) + [ANY] * len(held),
        out_specs=ANY,
        scratch_shapes=[pltpu.VMEM((2, h, w), F32), pltpu.SemaphoreType.DMA((STORES,))],
        input_output_aliases={1 + len(got): 0} if held else {},
        compiler_params=pltpu.CompilerParams(vmem_limit_bytes=LIMIT),
    )(base, *got, *held)


def on_device(spectrum, pupil, amplitudes, offsets, counts):
    w = pupil.shape[1]
    h = w // 2
    amp = amplitudes[0, 0, 0]
    offset = offsets[0, 0]

    def block(rows):
        return jax.ShapeDtypeStruct((2, rows, w), F32)

    half, whole, spot = block(h), block(w), block(EXTRA)
    pieces = [block(h // 2)] * 2
    (me,) = call(place_kernel, [spot], (), scalars=(offset,))
    head = spectrum[:, :h]
    tail = [spectrum[:, h : h + h // 2], spectrum[:, h + h // 2 :]]

    def each(values, axis, steps):
        return [shifted(value, axis, steps) for value in values]

    head_below = shifted(head, "row", -1)
    tail_right = each(tail, "col", -1)
    above = shifted(me, "row", 1)
    left_of = shifted(me, "col", 1)

    cosine, sine = dft_tables(w)
    square = jax.ShapeDtypeStruct((2 * w, 2 * w), BF16)
    stack = jax.ShapeDtypeStruct((2 * w, w), BF16)
    bx, bxt, by, byt_head, byt_tail, rolled = call(
        prepare_kernel, [square] * 3 + [stack] * 2 + [whole], (cosine, sine, pupil), scalars=(offset,)
    )

    (tail_made,) = call(
        functools.partial(compose_kernel, h, False), [block(h + EXTRA)], (me, above, tail, tail_right)
    )
    tail_both = shifted(tail_made, "row", -1)
    (head_made,) = call(
        functools.partial(compose_kernel, 0, True),
        [[pieces[0], block(h // 2 + EXTRA)]],
        (me, left_of, head, head_below),
        after=(tail_made,),
    )
    head_both = each(head_made, "col", -1)

    total = jax.ShapeDtypeStruct((2 * w, w), F32)
    products = pltpu.VMEM((w, w), BF16)
    left_half, left_whole = pltpu.VMEM((h, 2 * w), BF16), pltpu.VMEM((w, 2 * w), BF16)
    head_kept, acc, right_of = call(
        functools.partial(open_first, 0),
        [half, total, spot],
        (me, head, head_below, head_both, rolled, bx, byt_head),
        (left_half, products),
    )
    tail_kept, under, stacked, head_grad = call(
        functools.partial(close_first, h),
        [half, spot, stack, block(h + PAD)],
        (me, tail, tail_right, tail_both, acc, rolled, amp, bx, byt_tail, bxt, by),
        (left_whole, products),
        scalars=(counts,),
    )

    got_pairs = [swapped(head_grad, "row", False), swapped(head_grad, "row", True)]
    (tail_grad,) = call(functools.partial(rest_first, h), [[half]], (by, stacked, rolled))
    got_left, got_right = each(tail_grad, "col", 1), each(tail_grad, "col", -1)
    to_even, to_odd = call(
        functools.partial(between_kernel, h, False),
        [block(h + PAD), block(h + PAD)],
        (me, left_of, right_of, above, under, tail_grad, got_left, got_right),
    )
    (tail_own,) = call(
        functools.partial(own_kernel, h, False),
        [half],
        (me, left_of, right_of, tail_grad, got_left, got_right),
        after=(to_even,),
    )
    tail_sums = (tail_own, swapped(to_even, "row", False), swapped(to_odd, "row", True))
    to_left, to_right = call(
        functools.partial(between_kernel, 0, True),
        [[half], [half]],
        (me, above, under, left_of, right_of, head_grad, *got_pairs),
        after=(to_even,),
    )
    (head_own,) = call(
        functools.partial(own_kernel, 0, True),
        [half],
        (me, above, under, head_grad, *got_pairs),
        after=(to_left[0],),
    )
    head_sums = (head_own, each(to_right, "col", 1), each(to_left, "col", -1))

    (acc,) = call(
        functools.partial(open_second, 0),
        [total],
        (me, under, right_of, head_kept, *head_sums, rolled, bx, byt_head),
        (left_half, products),
    )
    stacked, head_total = call(
        functools.partial(close_second, h),
        [stack, half],
        (me, under, right_of, tail_kept, *tail_sums, acc, rolled, amp, bx, byt_tail, bxt, by, head_grad),
        (left_whole, products),
        scalars=(counts,),
    )

    head_above = shifted(head_total, "row", 1)
    (tail_total,) = call(
        functools.partial(rest_second, h), [pieces], (by, stacked, rolled, tail_grad)
    )
    tail_left = each(tail_total, "col", 1)
    tail_down, tail_base = call(
        functools.partial(final_kernel, h, False), [half, half], (me, left_of, tail, tail_total, tail_left)
    )
    tail_got = shifted(tail_down, "row", 1)
    head_right, head_base = call(
        functools.partial(final_kernel, 0, True),
        [pieces, half],
        (me, above, head, head_total, head_above),
        after=(tail_down,),
    )
    head_got = each(head_right, "col", 1)
    partial = store(0, head_base, head_got, whole)
    return store(h, tail_base, tail_got, whole, partial)


def solution(mesh):
    in_specs = (
        P(None, "row", "col"),
        P(),
        P("row", "col", None, None, None),
        P("row", "col", None, None),
        P("row", "col"),
    )
    out_specs = P(None, "row", "col")
    return jax.shard_map(
        on_device, mesh=mesh, in_specs=in_specs, out_specs=out_specs, check_vma=False
    )
```

```python
import functools
import math

import jax
import jax.numpy as jnp
from jax import lax
from jax.experimental import pallas as pl
from jax.experimental.pallas import tpu as pltpu
from jax.sharding import PartitionSpec as P

STEP = 0.5
FLOOR = 0.05
VMEM = pl.BlockSpec(memory_space=pltpu.VMEM)
ANY = pl.BlockSpec(memory_space=pl.ANY)
SMEM = pl.BlockSpec(memory_space=pltpu.SMEM)
LIMIT = 12 * 1024 * 1024
F32 = jnp.float32
BF16 = jnp.bfloat16

EXTRA = 8
BLOCK = 128
STORES = 4
ODD = 1024
PAD = 8


def shifted(value, axis, steps):
    count = lax.axis_size(axis)
    leading, last = (max(0, -steps), min(count, count - steps))
    return lax.ppermute(value, axis, [(source, source + steps) for source in range(leading, last)])


def swapped(value, axis, odd):
    lower = range(1 if odd else 0, lax.axis_size(axis) - 1, 2)
    return lax.ppermute(value, axis, [(a, a + 1) for a in lower] + [(a + 1, a) for a in lower])


def dft_tables(width):
    index = jnp.arange(width, dtype=jnp.int32)
    phase = index[:, None] * index[None, :] % width
    angle = phase.astype(jnp.float32) * (2.0 * math.pi / width)
    scale = 1.0 / math.sqrt(width)
    return (
        (jnp.cos(angle) * scale).astype(jnp.bfloat16),
        (jnp.sin(angle) * scale).astype(jnp.bfloat16),
    )


def call(kernel, outs, arrays, scratch=(), scalars=(), after=()):
    flat, tree = jax.tree.flatten(tuple(arrays))
    out_flat, out_tree = jax.tree.flatten(tuple(outs))
    skip, count = len(after), len(scalars)

    def body(*refs):
        refs = refs[skip:]
        numbers, refs = refs[:count], refs[count:]
        given = jax.tree.unflatten(tree, refs[: len(flat)])
        made = jax.tree.unflatten(out_tree, refs[len(flat) : len(flat) + len(out_flat)])
        kernel(*numbers, *given, *made, *refs[len(flat) + len(out_flat) :])

    results = pl.pallas_call(
        body,
        out_shape=out_flat,
        in_specs=[ANY] * skip + [SMEM] * count + [VMEM] * len(flat),
        out_specs=[VMEM] * len(out_flat),
        scratch_shapes=list(scratch),
        compiler_params=pltpu.CompilerParams(vmem_limit_bytes=LIMIT),
    )(*after, *scalars, *flat)
    return jax.tree.unflatten(out_tree, results)


def split(first, width):
    return [(first + row, slice(row, row + BLOCK)) for row in range(0, width // 2, BLOCK)]


def place_in(half, rows, width):
    if not isinstance(half, list):
        return half, rows
    height = width // 2 // len(half)
    index = rows.start // height
    return half[index], slice(rows.start - index * height, rows.stop - index * height)


def part(half, plane, rows, width):
    array, inner = place_in(half, rows, width)
    return array[plane, inner, :]


def put(half, plane, rows, value):
    array, inner = place_in(half, rows, value.shape[1])
    array[plane, inner, :] = value


def indices(rows, width, first):
    shape = (rows.stop - rows.start, width)
    return (
        lax.broadcasted_iota(jnp.int32, shape, 0) + first,
        lax.broadcasted_iota(jnp.int32, shape, 1),
    )


def low(i, place):
    return i + 1 < (place[0, :1, :].astype(jnp.int32) & (ODD - 1))


def far(j, place):
    return j + 1 < place[1, :1, :].astype(jnp.int32)


def ways_of(head, rows, width, first):
    i, j = indices(rows, width, first)
    pair = (functools.partial(low, i), functools.partial(far, j))
    return pair if head else pair[::-1]


def odd_row(place):
    return place[0, :1, :] >= ODD


def absent(place):
    return place[0, :1, :] == 0.0


def place_kernel(offset, out):
    odd = lax.rem(lax.axis_index("row"), 2) * ODD
    for plane, add in ((0, odd), (1, 0)):
        out[plane] = jnp.full(out.shape[1:], offset[0, plane] + 1 + add, jnp.int32).astype(F32)


def prepare_kernel(offset, cos_ref, sin_ref, pupil_ref, bx, bxt, by, byt_head, byt_tail, pupil_out):
    w = cos_ref.shape[0]
    h = w // 2
    cosine = cos_ref[...].astype(F32)
    sine = sin_ref[...].astype(F32)
    oy, ox = offset[0, 0], offset[0, 1]

    def rolled(value, shift, axis):
        return pltpu.roll(value, shift, axis)

    c, s = rolled(cosine, ox, 0).astype(BF16), rolled(sine, ox, 0).astype(BF16)
    bx[:w, :w], bx[:w, w:], bx[w:, :w], bx[w:, w:] = c, s, -s, c
    c, s = rolled(cosine, ox, 1).astype(BF16), rolled(sine, ox, 1).astype(BF16)
    bxt[:w, :w], bxt[:w, w:], bxt[w:, :w], bxt[w:, w:] = c, -s, s, c
    c, s = rolled(cosine, oy, 0).astype(BF16), rolled(sine, oy, 0).astype(BF16)
    by[:w, :w], by[:w, w:], by[w:, :w], by[w:, w:] = c, s, -s, c
    c, s = rolled(cosine, oy, 1).astype(BF16), rolled(sine, oy, 1).astype(BF16)
    for out, cols in ((byt_head, slice(0, h)), (byt_tail, slice(h, w))):
        n = cols.stop - cols.start
        out[:w, :n], out[:w, n:] = c[:, cols], -s[:, cols]
        out[w:, :n], out[w:, n:] = s[:, cols], c[:, cols]
    for plane in range(2):
        pupil_out[plane] = rolled(rolled(pupil_ref[plane], oy, 0), ox, 1)


def dot(a, b):
    return jnp.dot(a, b, preferred_element_type=F32)


def right_product(first, window, pupil, bx, left, half):
    w = bx.shape[0] // 2
    h = half.shape[0] // 2
    for row, rows in split(first, w):
        wr, wi = window(row, rows)
        across = slice(row, row + rows.stop - rows.start)
        pr, pi = pupil[0, across, :], pupil[1, across, :]
        left[rows, :w] = (wr * pr - wi * pi).astype(BF16)
        left[rows, w:] = (wr * pi + wi * pr).astype(BF16)
    half[:h, :] = dot(left[:h, :], bx[:, :w]).astype(BF16)
    half[h:, :] = dot(left[:h, :], bx[:, w:]).astype(BF16)


def finish(acc, byt_tail, half, amp, live, bxt, left, stacked):
    w = amp.shape[0]
    block = 256
    alive = (live[0, 0] > 0).astype(F32)
    for first in range(0, w, block):
        rows = slice(first, first + block)
        lower = slice(w + first, w + first + block)
        wave_r = acc[rows, :] + dot(byt_tail[rows, :], half[...])
        wave_i = acc[lower, :] + dot(byt_tail[lower, :], half[...])
        power = jnp.maximum(wave_r * wave_r + wave_i * wave_i, FLOOR * FLOOR)
        keep = (1.0 - amp[rows, :] * lax.rsqrt(power)) * alive
        left[rows, :w] = (wave_r * keep).astype(BF16)
        left[rows, w:] = (wave_i * keep).astype(BF16)
    stacked[:w, :] = dot(left[...], bxt[:, :w]).astype(BF16)
    stacked[w:, :] = dot(left[...], bxt[:, w:]).astype(BF16)


def back(first, by, stacked, pupil, out, extra):
    w = stacked.shape[1]
    h = w // 2
    back_r = dot(by[first : first + h, :], stacked[...])
    back_i = dot(by[w + first : w + first + h, :], stacked[...])
    for row, rows in split(first, w):
        across = slice(row, row + rows.stop - rows.start)
        pr, pi = pupil[0, across, :], pupil[1, across, :]
        br, bi = back_r[rows, :], back_i[rows, :]
        grad_r = br * pr + bi * pi
        grad_i = bi * pr - br * pi
        if extra is not None:
            grad_r = grad_r + part(extra, 0, rows, w)
            grad_i = grad_i + part(extra, 1, rows, w)
        put(out, 0, rows, grad_r)
        put(out, 1, rows, grad_i)


def gathered(head, place, tile, one, both, kept):
    w = kept.shape[2]

    def window(row, rows):
        first_way, second_way = ways_of(head, rows, w, row)
        a, b = first_way(place), second_way(place)
        values = []
        for plane in range(2):
            near = jnp.where(a, part(one, plane, rows, w), part(tile, plane, rows, w))
            value = jnp.where(b, part(both, plane, rows, w), near)
            kept[plane, rows, :] = value
            values.append(value)
        return values

    return window


def updated(head, place, edge_row, edge_col, kept, own, minus, plus):
    odd = odd_row(place)
    w = kept.shape[2]

    def window(row, rows):
        i, j = indices(rows, w, row)
        a, b = low(i, place), far(j, place)
        outside = (a & absent(edge_row)) | (b & absent(edge_col))
        second = b if head else a
        values = []
        for plane in range(2):
            low_side, high_side = part(minus, plane, rows, w), part(plus, plane, rows, w)
            if not head:
                low_side, high_side = pick(odd, low_side, high_side), pick(odd, high_side, low_side)
            near = jnp.where(second, high_side, low_side)
            value = kept[plane, rows, :] - STEP * (own[plane, rows, :] + near)
            values.append(jnp.where(outside, 0.0, value))
        return values

    return window


def open_first(first, place, tile, one, both, pupil, bx, byt, kept, acc, right_of, left, half):
    right_product(first, gathered(True, place, tile, one, both, kept), pupil, bx, left, half)
    acc[...] = dot(byt[...], half[...])
    right_of[...] = both[-1][:, both[-1].shape[1] - EXTRA :, :]


def close_first(
    first, live, place, tile, one, both, acc, pupil, amp, bx, byt, bxt, by, kept, under, stacked, out, left, half
):
    right_product(first, gathered(False, place, tile, one, both, kept), pupil, bx, left, half)
    finish(acc, byt, half, amp, live, bxt, left, stacked)
    back(0, by, stacked, pupil, out, None)
    under[...] = both[:, both.shape[1] - EXTRA :, :]


def open_second(
    first, place, edge_row, edge_col, kept, own, minus, plus, pupil, bx, byt, acc, left, half
):
    window = updated(True, place, edge_row, edge_col, kept, own, minus, plus)
    right_product(first, window, pupil, bx, left, half)
    acc[...] = dot(byt[...], half[...])


def close_second(
    first, live, place, edge_row, edge_col, kept, own, minus, plus, acc, pupil, amp, bx, byt, bxt, by,
    extra, stacked, out, left, half
):
    window = updated(False, place, edge_row, edge_col, kept, own, minus, plus)
    right_product(first, window, pupil, bx, left, half)
    finish(acc, byt, half, amp, live, bxt, left, stacked)
    back(0, by, stacked, pupil, out, extra)


def rest_first(first, by, stacked, pupil, out):
    back(first, by, stacked, pupil, out, None)


def rest_second(first, by, stacked, pupil, extra, out):
    back(first, by, stacked, pupil, out, extra)


def compose_kernel(first, head, me, target, tile, one, out):
    w = me.shape[2]
    for row, rows in split(first, w):
        mask = ways_of(head, rows, w, row)[0](target)
        for plane in range(2):
            value = jnp.where(mask, part(one, plane, rows, w), part(tile, plane, rows, w))
            put(out, plane, rows, value)
    end = out[-1] if head else out
    end[:, end.shape[1] - EXTRA :, :] = me[...]


def pick(odd, when_odd, when_even):
    return jnp.where(odd, when_odd, when_even)


def between(
    first, head, me, minus, plus, target_minus, target_plus, mine, got_minus, got_plus, to_minus, to_plus
):
    w = me.shape[2]
    for row, rows in split(first, w):
        ways = ways_of(head, rows, w, row)
        f, f_minus, f_plus = (ways[0](x) for x in (me, minus, plus))
        s, s_minus, s_plus = (ways[1](x) for x in (me, minus, plus))

        def seen(goal):
            return f == goal, ~goal & f_minus, goal & ~f_plus

        minus_m = [a & ~b for a, b in zip(seen(ways[0](target_minus)), (s, s_minus, s_plus))]
        plus_m = [a & b for a, b in zip(seen(ways[0](target_plus)), (s, s_minus, s_plus))]
        for plane in range(2):
            values = [part(x, plane, rows, w) for x in (mine, got_minus, got_plus)]
            sums = []
            for masks in (minus_m, plus_m):
                terms = [jnp.where(m, v, 0.0) for m, v in zip(masks, values)]
                sums.append(terms[0] + terms[1] + terms[2])
            put(to_minus, plane, rows, sums[0])
            put(to_plus, plane, rows, sums[1])


def by_parity(when_odd, when_even):
    odd = lax.rem(lax.axis_index("row"), 2) == 1
    pl.when(odd)(when_odd)
    pl.when(jnp.logical_not(odd))(when_even)


def between_kernel(
    first, head, me, minus, plus, target_minus, target_plus, mine, got_one, got_two, to_one, to_two
):
    places = (me, minus, plus, target_minus, target_plus, mine)
    if head:
        by_parity(
            lambda: between(first, head, *places, got_one, got_two, to_one, to_two),
            lambda: between(first, head, *places, got_two, got_one, to_one, to_two),
        )
    else:
        by_parity(
            lambda: between(first, head, *places, got_one, got_two, to_one, to_two),
            lambda: between(first, head, *places, got_one, got_two, to_two, to_one),
        )


def own_kernel(first, head, me, minus, plus, mine, got_minus, got_plus, own):
    w = me.shape[2]
    odd = odd_row(me)
    for row, rows in split(first, w):
        ways = ways_of(head, rows, w, row)
        f, f_minus, f_plus = (ways[0](x) for x in (me, minus, plus))
        s, s_minus, s_plus = (ways[1](x) for x in (me, minus, plus))
        own_minus, own_plus = ~f & f_minus & (s == s_minus), f & ~f_plus & (s == s_plus)
        for plane in range(2):
            values = [part(x, plane, rows, w) for x in (mine, got_minus, got_plus)]
            if head:
                values[1:] = pick(odd, values[1], values[2]), pick(odd, values[2], values[1])
            others = jnp.where(own_minus, values[1], 0.0) + jnp.where(own_plus, values[2], 0.0)
            put(own, plane, rows, values[0] + others)


def final_kernel(first, head, me, minus, tile, mine, got, to_plus, base):
    w = me.shape[2]
    for row, rows in split(first, w):
        ways = ways_of(head, rows, w, row)
        f, f_minus = ways[0](me), ways[0](minus)
        s, s_minus = ways[1](me), ways[1](minus)
        for plane in range(2):
            own = jnp.where(f, 0.0, part(mine, plane, rows, w))
            other = jnp.where(f_minus, part(got, plane, rows, w), 0.0)
            put(to_plus, plane, rows, jnp.where(s, own, 0.0) + jnp.where(s_minus, other, 0.0))
            kept = jnp.where(s, 0.0, own) + jnp.where(s_minus, 0.0, other)
            base[plane, rows, :] = part(tile, plane, rows, w) - STEP * kept


def store(first, base, got, whole, previous=None):
    _, h, w = base.shape
    held = () if previous is None else (previous,)
    got = got if isinstance(got, list) else [got]

    def kernel(base, *refs):
        pieces = refs[: len(got)]
        out, value, sems = refs[-3:]
        copies = []
        for k in range(STORES):
            size = h // STORES
            rows = slice(k * size, (k + 1) * size)
            for plane in range(2):
                value[plane, rows, :] = base[plane, rows, :] - STEP * part(list(pieces), plane, rows, w)
            copy = pltpu.make_async_copy(
                value.at[:, pl.ds(k * size, size), :], out.at[:, pl.ds(first + k * size, size), :], sems.at[k]
            )
            copy.start()
            copies.append(copy)
        for copy in copies:
            copy.wait()

    return pl.pallas_call(
        kernel,
        out_shape=whole,
        in_specs=[VMEM] * (1 + len(got)) + [ANY] * len(held),
        out_specs=ANY,
        scratch_shapes=[pltpu.VMEM((2, h, w), F32), pltpu.SemaphoreType.DMA((STORES,))],
        input_output_aliases={1 + len(got): 0} if held else {},
        compiler_params=pltpu.CompilerParams(vmem_limit_bytes=LIMIT),
    )(base, *got, *held)


def on_device(spectrum, pupil, amplitudes, offsets, counts):
    w = pupil.shape[1]
    h = w // 2
    amp = amplitudes[0, 0, 0]
    offset = offsets[0, 0]

    def block(rows):
        return jax.ShapeDtypeStruct((2, rows, w), F32)

    half, whole, spot = block(h), block(w), block(EXTRA)
    pieces = [block(h // 2)] * 2
    (me,) = call(place_kernel, [spot], (), scalars=(offset,))
    head = spectrum[:, :h]
    tail = [spectrum[:, h : h + h // 2], spectrum[:, h + h // 2 :]]

    def each(values, axis, steps):
        return [shifted(value, axis, steps) for value in values]

    head_below = shifted(head, "row", -1)
    tail_right = each(tail, "col", -1)
    above = shifted(me, "row", 1)
    left_of = shifted(me, "col", 1)

    cosine, sine = dft_tables(w)
    square = jax.ShapeDtypeStruct((2 * w, 2 * w), BF16)
    stack = jax.ShapeDtypeStruct((2 * w, w), BF16)
    bx, bxt, by, byt_head, byt_tail, rolled = call(
        prepare_kernel, [square] * 3 + [stack] * 2 + [whole], (cosine, sine, pupil), scalars=(offset,)
    )

    (tail_made,) = call(
        functools.partial(compose_kernel, h, False), [block(h + EXTRA)], (me, above, tail, tail_right)
    )
    tail_both = shifted(tail_made, "row", -1)
    (head_made,) = call(
        functools.partial(compose_kernel, 0, True),
        [[pieces[0], block(h // 2 + EXTRA)]],
        (me, left_of, head, head_below),
        after=(tail_made,),
    )
    head_both = each(head_made, "col", -1)

    total = jax.ShapeDtypeStruct((2 * w, w), F32)
    products = pltpu.VMEM((w, w), BF16)
    left_half, left_whole = pltpu.VMEM((h, 2 * w), BF16), pltpu.VMEM((w, 2 * w), BF16)
    head_kept, acc, right_of = call(
        functools.partial(open_first, 0),
        [half, total, spot],
        (me, head, head_below, head_both, rolled, bx, byt_head),
        (left_half, products),
    )
    tail_kept, under, stacked, head_grad = call(
        functools.partial(close_first, h),
        [half, spot, stack, block(h + PAD)],
        (me, tail, tail_right, tail_both, acc, rolled, amp, bx, byt_tail, bxt, by),
        (left_whole, products),
        scalars=(counts,),
    )

    got_pairs = [swapped(head_grad, "row", False), swapped(head_grad, "row", True)]
    (tail_grad,) = call(functools.partial(rest_first, h), [[half]], (by, stacked, rolled))
    got_left, got_right = each(tail_grad, "col", 1), each(tail_grad, "col", -1)
    to_even, to_odd = call(
        functools.partial(between_kernel, h, False),
        [block(h + PAD), block(h + PAD)],
        (me, left_of, right_of, above, under, tail_grad, got_left, got_right),
    )
    (tail_own,) = call(
        functools.partial(own_kernel, h, False),
        [half],
        (me, left_of, right_of, tail_grad, got_left, got_right),
        after=(to_even,),
    )
    tail_sums = (tail_own, swapped(to_even, "row", False), swapped(to_odd, "row", True))
    to_left, to_right = call(
        functools.partial(between_kernel, 0, True),
        [[half], [half]],
        (me, above, under, left_of, right_of, head_grad, *got_pairs),
        after=(to_even,),
    )
    (head_own,) = call(
        functools.partial(own_kernel, 0, True),
        [half],
        (me, above, under, head_grad, *got_pairs),
        after=(to_left[0],),
    )
    head_sums = (head_own, each(to_right, "col", 1), each(to_left, "col", -1))

    (acc,) = call(
        functools.partial(open_second, 0),
        [total],
        (me, under, right_of, head_kept, *head_sums, rolled, bx, byt_head),
        (left_half, products),
    )
    stacked, head_total = call(
        functools.partial(close_second, h),
        [stack, half],
        (me, under, right_of, tail_kept, *tail_sums, acc, rolled, amp, bx, byt_tail, bxt, by, head_grad),
        (left_whole, products),
        scalars=(counts,),
    )

    head_above = shifted(head_total, "row", 1)
    (tail_total,) = call(
        functools.partial(rest_second, h), [pieces], (by, stacked, rolled, tail_grad)
    )
    tail_left = each(tail_total, "col", 1)
    tail_down, tail_base = call(
        functools.partial(final_kernel, h, False), [block(h + PAD), half], (me, left_of, tail, tail_total, tail_left)
    )
    tail_got = shifted(tail_down, "row", 1)
    head_right, head_base = call(
        functools.partial(final_kernel, 0, True),
        [[half], half],
        (me, above, head, head_total, head_above),
        after=(tail_down,),
    )
    head_got = each(head_right, "col", 1)
    partial = store(0, head_base, head_got, whole)
    return store(h, tail_base, tail_got, whole, partial)


def solution(mesh):
    in_specs = (
        P(None, "row", "col"),
        P(),
        P("row", "col", None, None, None),
        P("row", "col", None, None),
        P("row", "col"),
    )
    out_specs = P(None, "row", "col")
    return jax.shard_map(
        on_device, mesh=mesh, in_specs=in_specs, out_specs=out_specs, check_vma=False
    )
```
